256 devices in a mesh: leaf: 64 (over y, z, core), rows: 4 (over x).
Axes of the slice: x: 4, y: 4, z: 8, core: 2. Of those that a mesh axis runs over, the one named last changes fastest.
Arguments:
- mixing: bfloat16 [192, 1024, 1024], P('leaf'), may hold values from 0.04 to 2048
- emission: bfloat16 [192, 256, 1024], P('leaf'), may hold values from 0.099609375 to 10
- prior: float32 [1024], replicated, may hold values from 0.1 to 10
- parent: int32 [192], P('leaf'), may hold values from -1 to 191, as said below
- observed: int32 [192, 512], P('leaf', 'rows'), may hold values from 0 to 255
Outputs:
- pair_counts: bfloat16 [192, 1024, 1024], P('leaf', 'rows')
- emit_counts: bfloat16 [192, 256, 1024], P('leaf', None, 'rows')
The draws below stay inside these ranges and needn't reach their ends.
Inputs may be any that keep to these rules, and one draw needn't show every extreme that they name: Nodes are numbered 3 to an index of leaf, in order. Every parent has a smaller number than its child. A node that is not the first of its index of leaf has its parent among the nodes of the same index. The first node of index d > 0 has as parent the first node of index d with its lowest set binary digit cleared. Node 0 is the root.
All inputs are finite; a program needn't handle non-finite values.
Results may differ from the reference program's by a relative error of at most 0.009.
Values may be sent and summed in bfloat16 or wider, within the bound.
A program may use at most 128 MiB of HBM per device.

```python
import math
import jax
import jax.numpy as jnp
from jax import lax

K = 1024
V = 256
NODE_DEV = 3
NODES = 192
SAMPLES = 512


def draw_mixing(key, part):
    keys = jax.random.split(jax.random.fold_in(key, 11), NODES)

    def single(node_key):
        first, second = jax.random.split(node_key)
        spread = jnp.exp(jax.random.uniform(first, (K, K), jnp.float32, math.log(0.05), 0.0))
        share = jax.random.uniform(second, (K,), jnp.float32, 0.25, 1.0)
        bump = jnp.sum(spread, axis=1) * share
        return spread + jnp.eye(K, dtype=jnp.float32) * bump[:, None]
    return lax.map(single, keys).astype(jnp.bfloat16)


def draw_parent(key, part):
    index = jnp.arange(NODES, dtype=jnp.int32)
    holder = index // NODE_DEV
    local = index % NODE_DEV
    pick = jax.random.randint(jax.random.fold_in(key, 7), (NODES,), 0, jnp.maximum(local, 1), dtype=jnp.int32)
    inside = holder * NODE_DEV + pick
    upper = jnp.bitwise_and(holder, holder - 1) * NODE_DEV
    return jnp.where(local > 0, inside, jnp.where(holder > 0, upper, -1)).astype(jnp.int32)


def touch_ends(entries, rng, low, largest):
    extent = entries.shape
    spot = [jax.random.randint(jax.random.fold_in(rng, axis), (), 0, extent[axis]) for axis in range(len(extent))]
    entries = entries.at[tuple(spot)].set(low)
    longest = extent.index(max(extent))
    spot[longest] = (spot[longest] + 1) % extent[longest]
    return entries.at[tuple(spot)].set(largest)


def shard_levels(rng, dims, cuts, least, largest):
    def one(position, parts):
        draws = jax.random.uniform(jax.random.fold_in(jax.random.fold_in(rng, 6), position), (parts,), jnp.float32, least / len(cuts), largest / len(cuts))
        return jnp.repeat(jnp.exp(draws), dims[position] // parts).reshape((-1,) + (1,) * (len(dims) - position - 1))

    gain = one(*cuts[0])
    for cut in cuts[1:]:
        gain = gain * one(*cut)
    return gain


def setup_inputs(seed: int = 0) -> dict:
    streams_of = jax.random.split(jax.random.key(seed), 6)
    mixing = draw_mixing(jax.random.fold_in(streams_of[5], 71), 0)
    emission = jnp.clip(jnp.exp(math.log(10.0) - 4.609084 * jax.random.uniform(streams_of[1], (NODES, V, K), jnp.float32) ** shard_levels(streams_of[1], (NODES, V, K), ((0, 64),), -0.2, 0.2)), 0.099609375, 10.0).astype(jnp.bfloat16)
    prior = jnp.clip(jnp.exp(jax.random.uniform(streams_of[2], (K,), jnp.float32, math.log(0.1), math.log(10.0))), 0.1, 10.0)
    parent = draw_parent(jax.random.fold_in(streams_of[5], 71), 0)
    observed = touch_ends(jax.random.randint(streams_of[4], (NODES, SAMPLES), 0, V), jax.random.fold_in(streams_of[4], 1), 0, V - 1).astype(jnp.int32)
    return dict(mixing=mixing, emission=emission, prior=prior, parent=parent, observed=observed)


def node_weights(raw_rows):
    wide = raw_rows.astype(jnp.float32)
    return (wide / jnp.sum(wide, axis=1, keepdims=True)).astype(jnp.bfloat16)


def node_table(raw_table):
    wide = raw_table.astype(jnp.float32)
    return (wide / jnp.sum(wide, axis=0, keepdims=True)).astype(jnp.bfloat16)


def one_hot_rows(values):
    return (values[:, None] == jnp.arange(V, dtype=jnp.int32)[None, :]).astype(jnp.bfloat16)


def outgoing(lam, weight):
    return lax.dot_general(lam, weight, (((1,), (1,)), ((), ())), preferred_element_type=jnp.float32)


def reference(mixing, emission, prior, parent, observed):
    prods = jnp.ones((NODES, SAMPLES, K), jnp.float32)
    lams = jnp.zeros((NODES, SAMPLES, K), jnp.bfloat16)
    root_msg = jnp.ones((SAMPLES, K), jnp.float32)

    def up_step(i, state):
        prods, lams, root_msg = state
        node = (NODES - 1 - i).astype(jnp.int32)
        weight = node_weights(mixing[node])
        hot = one_hot_rows(observed[node])
        emit = jnp.dot(hot, node_table(emission[node]), preferred_element_type=jnp.float32)
        raw = emit * prods[node]
        scale = jnp.mean(raw, axis=1, keepdims=True)
        lam = (raw / scale).astype(jnp.bfloat16)
        msg = outgoing(lam, weight)
        above = parent[node]
        target = jnp.maximum(above, 0).astype(jnp.int32)
        updated = jnp.where(above >= 0, prods[target] * msg, prods[target])
        prods = prods.at[target].set(updated)
        root_msg = jnp.where(above < 0, msg, root_msg)
        lams = lams.at[node].set(lam)
        return prods, lams, root_msg

    prods, lams, root_msg = lax.fori_loop(jnp.int32(0), jnp.int32(NODES), up_step, (prods, lams, root_msg))
    prior_share = prior / jnp.sum(prior)
    weighted = prior_share[None, :] * root_msg
    root_post = weighted / jnp.sum(weighted, axis=1, keepdims=True)
    pair = jnp.zeros((NODES, K, K), jnp.bfloat16)
    emit_c = jnp.zeros((NODES, V, K), jnp.bfloat16)
    pair_scale = K * K / SAMPLES
    emit_scale = V * K / SAMPLES

    def down_step(node, state):
        posts, pair, emit_c = state
        weight = node_weights(mixing[node])
        lam = lams[node]
        msg = outgoing(lam, weight)
        above = parent[node]
        source = jnp.maximum(above, 0).astype(jnp.int32)
        q_par = jnp.where(above >= 0, posts[source], root_post)
        ratio = (q_par / msg).astype(jnp.bfloat16)
        post = lam.astype(jnp.float32) * jnp.dot(ratio, weight, preferred_element_type=jnp.float32)
        posts = posts.at[node].set(post)
        flow = lax.dot_general(ratio, lam, (((0,), (0,)), ((), ())), preferred_element_type=jnp.float32)
        pair = pair.at[node].set((weight.astype(jnp.float32) * flow * pair_scale).astype(jnp.bfloat16))
        hot = one_hot_rows(observed[node])
        tally = lax.dot_general(hot, post.astype(jnp.bfloat16), (((0,), (0,)), ((), ())), preferred_element_type=jnp.float32)
        emit_c = emit_c.at[node].set((tally * emit_scale).astype(jnp.bfloat16))
        return posts, pair, emit_c

    posts, pair, emit_c = lax.fori_loop(jnp.int32(0), jnp.int32(NODES), down_step, (prods, pair, emit_c))
    return pair, emit_c
```

```python
import functools

import jax
import jax.numpy as jnp
from jax import lax
from jax.experimental import pallas as pl
from jax.experimental.pallas import tpu as pltpu
from jax.sharding import PartitionSpec as P

F32 = jnp.float32
BF16 = jnp.bfloat16
CHUNKS = 4
NB = 256


def dot_nt(a, b):
    return lax.dot_general(a, b, (((1,), (1,)), ((), ())), preferred_element_type=F32)


def dot_nn(a, b):
    return lax.dot_general(a, b, (((1,), (0,)), ((), ())), preferred_element_type=F32)


def dot_tn(a, b):
    return lax.dot_general(a, b, (((0,), (0,)), ((), ())), preferred_element_type=F32)


def kernel(
    levels,
    groups,
    mixing,
    emission,
    prior,
    parent,
    observed,
    pair_out,
    emit_out,
    A,
    em,
    lam_all,
    upart,
    m2,
    msg_in,
    m_out,
    macc,
    inv_row,
    q_in,
    h0,
    q0f,
    q1f,
    qb,
    hs0,
    qs,
    ginv,
    obs_all,
    oht,
    pair_v,
    emit_v,
    load_sem,
    up_send,
    up_recv,
    dn_send,
    dn_recv,
    ag_send,
    ag_recv,
    hx_send,
    hx_recv,
    q0_send,
    q0_recv,
    qx_send,
    qx_recv,
    ob_send,
    ob_recv,
    out_sem,
):
    K = A.shape[1]
    V = em.shape[1]
    R = upart.shape[0]
    Ks = K // groups
    C = CHUNKS
    S = R // C
    pair_scale = float(K * K // (R * groups))
    emit_scale = float(V * K // (R * groups))

    d = lax.axis_index("leaf")
    r = lax.axis_index("rows")
    lvl = jnp.int32(0)
    low = jnp.int32(1)
    for j in range(levels):
        zero = jnp.where(d % (2 ** (j + 1)) == 0, 1, 0)
        lvl = lvl + zero
        low = low + zero * (2**j)
    is_root = lvl == levels
    up_dev = jnp.where(is_root, d, d - low)
    own = pl.multiple_of(r * R, R)
    mine = pl.multiple_of(r * Ks, Ks)

    def peer(k):
        return lax.rem(r + k, groups)

    order = (2, 1, 0)
    loads = {}
    for n, g in enumerate(order):
        loads["e", g] = pltpu.make_async_copy(emission.at[g], em.at[g], load_sem.at[2 * n])
        loads["m", g] = pltpu.make_async_copy(mixing.at[g], A.at[g], load_sem.at[2 * n + 1])
        loads["e", g].start()
        loads["m", g].start()

    barrier = pltpu.get_barrier_semaphore()

    def greet(leaf, rows):
        pl.semaphore_signal(
            barrier,
            inc=1,
            device_id={"leaf": leaf, "rows": rows},
            device_id_type=pl.DeviceIdType.MESH,
        )

    @pl.when(jnp.logical_not(is_root))
    def _():
        greet(up_dev, r)

    def greet_child(j, step):
        greet(d + step, r)
        return step * 2

    lax.fori_loop(0, lvl, greet_child, jnp.int32(1))
    for k in range(1, groups):
        greet(d, peer(k))

    def arrived(ref, sem):
        pltpu.make_async_remote_copy(
            src_ref=ref,
            dst_ref=ref,
            send_sem=sem,
            recv_sem=sem,
            device_id={"leaf": d, "rows": peer(1)},
            device_id_type=pl.DeviceIdType.MESH,
        ).wait_recv()

    def up_copy(i):
        rows = pl.ds(pl.multiple_of(i * S, S), S)
        return pltpu.make_async_remote_copy(
            src_ref=m_out.at[rows],
            dst_ref=msg_in.at[jnp.minimum(lvl, levels - 1), rows],
            send_sem=up_send.at[i],
            recv_sem=up_recv.at[jnp.minimum(lvl, levels - 1), i],
            device_id={"leaf": up_dev, "rows": r},
            device_id_type=pl.DeviceIdType.MESH,
        )

    def wait_up(j, i):
        rows = pl.ds(pl.multiple_of(i * S, S), S)
        arrived(msg_in.at[j, rows], up_recv.at[j, i])

    def dn_copy(j, step, i):
        rows = pl.ds(pl.multiple_of(i * S, S), S)
        return pltpu.make_async_remote_copy(
            src_ref=qb.at[0, rows],
            dst_ref=q_in.at[rows],
            send_sem=dn_send.at[j, i],
            recv_sem=dn_recv.at[i],
            device_id={"leaf": d + step, "rows": r},
            device_id_type=pl.DeviceIdType.MESH,
        )

    def wait_dn(i):
        rows = pl.ds(pl.multiple_of(i * S, S), S)
        arrived(q_in.at[rows], dn_recv.at[i])

    def ag_copy(g, k):
        return pltpu.make_async_remote_copy(
            src_ref=lam_all.at[g, pl.ds(own, R)],
            dst_ref=lam_all.at[g, pl.ds(own, R)],
            send_sem=ag_send.at[g, k - 1],
            recv_sem=ag_recv.at[g, k - 1],
            device_id={"leaf": d, "rows": peer(k)},
            device_id_type=pl.DeviceIdType.MESH,
        )

    def ag_wait(g):
        for k in range(1, groups):
            src = pl.multiple_of(lax.rem(r + groups - k, groups) * R, R)
            arrived(lam_all.at[g, pl.ds(src, R)], ag_recv.at[g, k - 1])

    def slice_copy(src, dst, send_sem, recv_sem, k, row, count):
        to = peer(k)
        cols = pl.ds(pl.multiple_of(to * Ks, Ks), Ks)
        return pltpu.make_async_remote_copy(
            src_ref=src.at[pl.ds(row, count), cols],
            dst_ref=dst.at[pl.ds(pl.multiple_of(own + row, count), count)],
            send_sem=send_sem,
            recv_sem=recv_sem,
            device_id={"leaf": d, "rows": to},
            device_id_type=pl.DeviceIdType.MESH,
        )

    def slice_wait(dst, recv_sem, k, row, count):
        src = lax.rem(r + groups - k, groups) * R
        arrived(dst.at[pl.ds(pl.multiple_of(src + row, count), count)], recv_sem)

    def ob_copy(k):
        return pltpu.make_async_remote_copy(
            src_ref=observed,
            dst_ref=obs_all.at[r],
            send_sem=ob_send.at[k - 1],
            recv_sem=ob_recv.at[k - 1],
            device_id={"leaf": d, "rows": peer(k)},
            device_id_type=pl.DeviceIdType.MESH,
        )

    chain = parent[2] == d * 3 + 1
    ones = jnp.ones((16, K), BF16)
    values = lax.broadcasted_iota(jnp.int32, (V, R), 0)

    def emitted(g):
        loads["e", g].wait()
        hot = jnp.where(values == observed[g : g + 1, :], 1.0, 0.0).astype(BF16)
        table = em[g]
        column = jnp.sum(table.astype(F32), axis=0, keepdims=True)
        return dot_tn(hot, table) * (1.0 / column)

    def scaled(u):
        return (u / jnp.mean(u, axis=1, keepdims=True)).astype(BF16)

    def lift_local(g, u):
        lam = scaled(u)
        lam_all[g, pl.ds(own, R), :] = lam
        left = jnp.concatenate([lam, ones], axis=0)
        loads["m", g].wait()
        parts = []
        for n in range(K // NB):
            cols = slice(n * NB, (n + 1) * NB)
            acc = dot_nt(left, A[g, cols, :])
            macc[g, :, cols] = acc[:R]
            parts.append(acc[:R] * (1.0 / acc[R : R + 1]))
        return parts

    parts = lift_local(2, emitted(2))
    for n, part in enumerate(parts):
        m2[:, n * NB : (n + 1) * NB] = part
    parts = lift_local(1, emitted(1) * jnp.where(chain, m2[...], 1.0))
    for n, part in enumerate(parts):
        cols = slice(n * NB, (n + 1) * NB)
        upart[:, cols] = part * jnp.where(chain, 1.0, m2[:, cols])
    upart[...] = upart[...] * emitted(0)
    loads["m", 0].wait()

    pl.semaphore_wait(barrier, lvl + (groups - 1) + jnp.where(is_root, 0, 1))

    def aux():
        for k in range(1, groups):
            ob_copy(k).start()
        for g in (2, 1):
            for k in range(1, groups):
                ag_copy(g, k).start()
        for g in (2, 1):
            macc[g] = 1.0 / macc[g]

    @pl.when(lvl > 0)
    def _():
        aux()

    def early_child(j, carry):
        for i in range(C):
            wait_up(j, i)
        upart[...] = upart[...] * msg_in[j].astype(F32)
        return carry

    lax.fori_loop(0, lvl - 1, early_child, 0)

    def up(i):
        rows = pl.ds(pl.multiple_of(i * S, S), S)

        @pl.when(lvl > 0)
        def _():
            wait_up(lvl - 1, i)
            upart[rows, :] = upart[rows, :] * msg_in[lvl - 1, rows, :].astype(F32)

        lam = scaled(upart[rows, :])
        lam_all[0, pl.ds(pl.multiple_of(own + i * S, S), S), :] = lam
        acc = dot_nt(jnp.concatenate([lam, ones], axis=0), A[0])
        inverse = 1.0 / acc[S : S + 1]
        m_out[rows, :] = (acc[:S] * inverse).astype(BF16)

        @pl.when(jnp.logical_not(is_root))
        def _():
            up_copy(i).start()

        inv_row[0:1, :] = inverse
        macc[0, rows, :] = jnp.where(is_root, acc[:S], 1.0 / acc[:S])

    def down(i):
        row = pl.multiple_of(i * S, S)
        rows = pl.ds(row, S)

        @pl.when(is_root)
        def _():
            weight = (prior[...] / jnp.sum(prior[...], axis=1, keepdims=True)) * inv_row[0:1, :]
            total = jnp.sum(weight * macc[0, rows, :], axis=1, keepdims=True)
            h0[rows, :] = (weight / total).astype(BF16)

        @pl.when(jnp.logical_not(is_root))
        def _():
            wait_dn(i)
            h0[rows, :] = (q_in[rows, :].astype(F32) * macc[0, rows, :]).astype(BF16)

        h = h0[rows, :]
        lam = lam_all[0, pl.ds(pl.multiple_of(own + row, S), S), :].astype(F32)
        q = lam * dot_nn(h, A[0])
        qb[0, rows, :] = q.astype(BF16)

        def send_child(n, step):
            dn_copy(lvl - 1 - n, step, i).start()
            return step // 2

        lax.fori_loop(0, lvl, send_child, low // 2)
        for k in range(1, groups):
            slice_copy(h0, hs0, hx_send.at[k - 1, i], hx_recv.at[k - 1, i], k, row, S).start()
        for k in range(1, groups):
            slice_copy(
                qb.at[0], qs.at[0], q0_send.at[k - 1, i], q0_recv.at[k - 1, i], k, row, S
            ).start()
        q0f[rows, :] = q
        there = pl.ds(pl.multiple_of(own + row, S), S)
        hs0[there, :] = h0[rows, pl.ds(mine, Ks)]
        qs[0, there, :] = qb[0, rows, pl.ds(mine, Ks)]

    def middle():
        for k in range(1, groups):
            src = lax.rem(r + groups - k, groups)
            arrived(obs_all.at[src], ob_recv.at[k - 1])
        obs_all[r] = observed[...]
        for g in range(3):
            for n in range(groups):
                oht[g, :, n * R : (n + 1) * R] = jnp.where(
                    values == obs_all[n, g : g + 1, :], 1.0, 0.0
                ).astype(BF16)
        for g in (2, 1):
            ag_wait(g)
            block = A[g, pl.ds(mine, Ks), :]
            for n in range(groups):
                part = slice(n * R, (n + 1) * R)
                ginv[g - 1, part, :] = 1.0 / dot_nt(lam_all[g, part, :], block)

    early_mid = lvl <= 1
    mid_step = jnp.where(early_mid, C, 2 * C)

    def step(s, carry):
        is_mid = s == mid_step
        t = s - jnp.where(s > mid_step, 1, 0)
        is_up = jnp.where(is_root, t % 2 == 0, t < C)
        is_up = jnp.logical_and(is_up, jnp.logical_not(is_mid))
        is_down = jnp.logical_not(jnp.logical_or(is_up, is_mid))
        i = jnp.where(is_root, t // 2, t % C)
        i = jnp.where(is_mid, 0, i)

        @pl.when(is_up)
        def _():
            up(i)

            @pl.when(i == C - 1)
            def _():
                for k in range(1, groups):
                    ag_copy(0, k).start()

                @pl.when(lvl == 0)
                def _():
                    aux()

        @pl.when(is_mid)
        def _():
            middle()

        @pl.when(is_down)
        def _():
            down(i)

        return carry

    lax.fori_loop(0, 2 * C + 1, step, 0)

    def settle_local(g, q_par):
        h = (q_par * macc[g]).astype(BF16)
        lam = lam_all[g, pl.ds(own, R), :]
        out = []
        for n in range(K // NB):
            cols = slice(n * NB, (n + 1) * NB)
            q = lam[:, cols].astype(F32) * dot_nn(h, A[g, :, cols])
            qb[g, :, cols] = q.astype(BF16)
            if g == 1:
                q1f[:, cols] = q
        for k in range(1, groups):
            slice_copy(
                qb.at[g], qs.at[g], qx_send.at[g - 1, k - 1], qx_recv.at[g - 1, k - 1], k, 0, R
            ).start()
        qs[g, pl.ds(own, R), :] = qb[g, :, pl.ds(mine, Ks)]

    settle_local(1, q0f[...])
    settle_local(2, jnp.where(chain, q1f[...], q0f[...]))

    def finish(g, h):
        cells = dot_tn(h, lam_all[g])
        raw = A[g, pl.ds(mine, Ks), :].astype(F32)
        pair_v[g] = (raw * cells * pair_scale).astype(BF16)
        pltpu.make_async_copy(pair_v.at[g], pair_out.at[g], out_sem.at[g]).start()

    def tally(g):
        emit_v[g] = (dot_nn(oht[g], qs[g]) * emit_scale).astype(BF16)
        pltpu.make_async_copy(emit_v.at[g], emit_out.at[g], out_sem.at[3 + g]).start()

    ag_wait(0)
    for k in range(1, groups):
        for i in range(C):
            slice_wait(hs0, hx_recv.at[k - 1, i], k, i * S, S)
    finish(0, hs0[...])
    for k in range(1, groups):
        for i in range(C):
            slice_wait(qs.at[0], q0_recv.at[k - 1, i], k, i * S, S)
    h1 = (qs[0].astype(F32) * ginv[0]).astype(BF16)
    finish(1, h1)
    tally(0)
    for k in range(1, groups):
        slice_wait(qs.at[1], qx_recv.at[0, k - 1], k, 0, R)
    h2 = (jnp.where(chain, qs[1].astype(F32), qs[0].astype(F32)) * ginv[1]).astype(BF16)
    finish(2, h2)
    tally(1)
    for k in range(1, groups):
        slice_wait(qs.at[2], qx_recv.at[1, k - 1], k, 0, R)
    tally(2)

    @pl.when(jnp.logical_not(is_root))
    def _():
        for i in range(C):
            up_copy(i).wait_send()

    def drain_child(n, step):
        for i in range(C):
            dn_copy(lvl - 1 - n, step, i).wait_send()
        return step // 2

    lax.fori_loop(0, lvl, drain_child, low // 2)
    for k in range(1, groups):
        ob_copy(k).wait_send()
        for g in range(3):
            ag_copy(g, k).wait_send()
        for i in range(C):
            slice_copy(
                h0, hs0, hx_send.at[k - 1, i], hx_recv.at[k - 1, i], k, i * S, S
            ).wait_send()
            slice_copy(
                qb.at[0], qs.at[0], q0_send.at[k - 1, i], q0_recv.at[k - 1, i], k, i * S, S
            ).wait_send()
        for g in (1, 2):
            slice_copy(
                qb.at[g], qs.at[g], qx_send.at[g - 1, k - 1], qx_recv.at[g - 1, k - 1], k, 0, R
            ).wait_send()
    for g in range(3):
        pltpu.make_async_copy(pair_v.at[g], pair_out.at[g], out_sem.at[g]).wait()
        pltpu.make_async_copy(emit_v.at[g], emit_out.at[g], out_sem.at[3 + g]).wait()


def per_device(levels, groups, mixing, emission, prior, parent, observed):
    nodes, K, _ = mixing.shape
    V = emission.shape[1]
    R = observed.shape[1]
    Ks = K // groups
    T = groups * R
    C = CHUNKS
    dma = pltpu.SemaphoreType.DMA
    vmem = pltpu.VMEM
    return pl.pallas_call(
        functools.partial(kernel, levels, groups),
        out_shape=(
            jax.ShapeDtypeStruct((nodes, Ks, K), BF16),
            jax.ShapeDtypeStruct((nodes, V, Ks), BF16),
        ),
        in_specs=[
            pl.BlockSpec(memory_space=pl.ANY),
            pl.BlockSpec(memory_space=pl.ANY),
            pl.BlockSpec(memory_space=pltpu.VMEM),
            pl.BlockSpec(memory_space=pltpu.SMEM),
            pl.BlockSpec(memory_space=pltpu.VMEM),
        ],
        out_specs=(pl.BlockSpec(memory_space=pl.ANY), pl.BlockSpec(memory_space=pl.ANY)),
        scratch_shapes=[
            vmem((nodes, K, K), BF16),
            vmem((nodes, V, K), BF16),
            vmem((nodes, T, K), BF16),
            vmem((R, K), F32),
            vmem((R, K), F32),
            vmem((levels, R, K), BF16),
            vmem((R, K), BF16),
            vmem((nodes, R, K), F32),
            vmem((8, K), F32),
            vmem((R, K), BF16),
            vmem((R, K), BF16),
            vmem((R, K), F32),
            vmem((R, K), F32),
            vmem((nodes, R, K), BF16),
            vmem((T, Ks), BF16),
            vmem((nodes, T, Ks), BF16),
            vmem((2, T, Ks), F32),
            vmem((groups, nodes, R), jnp.int32),
            vmem((nodes, V, T), BF16),
            vmem((nodes, Ks, K), BF16),
            vmem((nodes, V, Ks), BF16),
            dma((6,)),
            dma((C,)),
            dma((levels, C)),
            dma((levels, C)),
            dma((C,)),
            dma((3, groups - 1)),
            dma((3, groups - 1)),
            dma((groups - 1, C)),
            dma((groups - 1, C)),
            dma((groups - 1, C)),
            dma((groups - 1, C)),
            dma((2, groups - 1)),
            dma((2, groups - 1)),
            dma((groups - 1,)),
            dma((groups - 1,)),
            dma((6,)),
        ],
        compiler_params=pltpu.CompilerParams(
            collective_id=0, has_side_effects=True, vmem_limit_bytes=60 * 1024 * 1024
        ),
        name="tree_pass",
    )(mixing, emission, prior.reshape(1, K), parent, observed)


def solution(mesh):
    levels = mesh.shape["leaf"].bit_length() - 1
    groups = mesh.shape["rows"]
    placed = (P("leaf", None, None), P("leaf", None, None), P(), P("leaf"), P("leaf", "rows"))
    return jax.shard_map(
        functools.partial(per_device, levels, groups),
        mesh=mesh,
        in_specs=placed,
        out_specs=(P("leaf", "rows", None), P("leaf", None, "rows")),
        check_vma=False,
    )
```

```python
import functools

import jax
import jax.numpy as jnp
from jax import lax
from jax.experimental import pallas as pl
from jax.experimental.pallas import tpu as pltpu
from jax.sharding import PartitionSpec as P

F32 = jnp.float32
BF16 = jnp.bfloat16
CHUNKS = 4
HALVES = 2
COST_FLOPS = 10**9
COST_BYTES = 10**7
VMEM_BYTES = 48_000_000
NB = 256


def dot_nt(a, b):
    return lax.dot_general(a, b, (((1,), (1,)), ((), ())), preferred_element_type=F32)


def dot_nn(a, b):
    return lax.dot_general(a, b, (((1,), (0,)), ((), ())), preferred_element_type=F32)


def dot_tn(a, b):
    return lax.dot_general(a, b, (((0,), (0,)), ((), ())), preferred_element_type=F32)


def kernel(
    levels,
    groups,
    mixing,
    emission,
    prior,
    parent,
    observed,
    pair_v,
    emit_v,
    A,
    A0T,
    em,
    lam_all,
    upart,
    m2,
    msg_in,
    m_out,
    macc,
    inv_row,
    q_in,
    h0,
    q0f,
    q1f,
    qb,
    qp,
    qs,
    relay,
    ginv,
    obs_all,
    oht,
    load_sem,
    up_send,
    up_recv,
    dn_send,
    dn_recv,
    ag_send,
    ag_recv,
    q0_send,
    q0_recv,
    qx_send,
    qx_recv,
    rl_send,
    rl_recv,
    qp_send,
    qp_recv,
    tp_send,
    tp_recv,
    ob_send,
    ob_recv,
):
    K = A.shape[1]
    V = em.shape[1]
    R = upart.shape[0]
    Ks = K // groups
    C = CHUNKS
    S = R // C
    H = HALVES
    W = K // H
    pair_scale = float(K * K // (R * groups))
    emit_scale = float(V * K // (R * groups))
    pieces = [(i, h) for i in range(C) for h in range(H)]

    d = lax.axis_index("leaf")
    r = lax.axis_index("rows")
    lvl = jnp.int32(0)
    low = jnp.int32(1)
    for j in range(levels):
        zero = jnp.where(d % (2 ** (j + 1)) == 0, 1, 0)
        lvl = lvl + zero
        low = low + zero * (2**j)
    is_root = lvl == levels
    odd = d % 2
    up_dev = jnp.where(is_root, d, d - low)
    slot = jnp.minimum(lvl, levels - 1)
    own = pl.multiple_of(r * R, R)
    mine = pl.multiple_of(r * Ks, Ks)

    def peer(k):
        return lax.rem(r + k, groups)

    def block(k):
        return pl.ds(pl.multiple_of(lax.rem(r + groups - k, groups) * R, R), R)

    loads = {}
    for n, g in enumerate((2, 1, 0)):
        loads["e", g] = pltpu.make_async_copy(emission.at[g], em.at[g], load_sem.at[2 * n])
        loads["m", g] = pltpu.make_async_copy(mixing.at[g], A.at[g], load_sem.at[2 * n + 1])
        loads["e", g].start()
        loads["m", g].start()

    barrier = pltpu.get_barrier_semaphore()

    def greet(leaf, rows):
        pl.semaphore_signal(
            barrier,
            inc=1,
            device_id={"leaf": leaf, "rows": rows},
            device_id_type=pl.DeviceIdType.MESH,
        )

    @pl.when(jnp.logical_not(is_root))
    def _():
        greet(up_dev, r)

    def greet_child(j, step):
        greet(d + step, r)
        return step * 2

    lax.fori_loop(0, lvl, greet_child, jnp.int32(1))
    for k in range(1, groups):
        greet(d, peer(k))

    def remote(src, dst, send_sem, recv_sem, leaf, rows):
        return pltpu.make_async_remote_copy(
            src_ref=src,
            dst_ref=dst,
            send_sem=send_sem,
            recv_sem=recv_sem,
            device_id={"leaf": leaf, "rows": rows},
            device_id_type=pl.DeviceIdType.MESH,
        )

    def arrived(ref, sem):
        remote(ref, ref, sem, sem, d, peer(1)).wait_recv()

    def spot(i, h):
        return pl.ds(pl.multiple_of(i * S, S), S), pl.ds(h * W, W)

    def up_copy(i, h):
        rows, cols = spot(i, h)
        return remote(
            m_out.at[rows, cols],
            msg_in.at[slot, rows, cols],
            up_send.at[i, h],
            up_recv.at[slot, i, h],
            up_dev,
            r,
        )

    def wait_up(j, i):
        for h in range(H):
            rows, cols = spot(i, h)
            arrived(msg_in.at[j, rows, cols], up_recv.at[j, i, h])

    def dn_copy(j, step, i, h):
        rows, cols = spot(i, h)
        return remote(
            qb.at[0, rows, cols],
            q_in.at[rows, cols],
            dn_send.at[j, i, h],
            dn_recv.at[i, h],
            d + step,
            r,
        )

    def wait_dn(i):
        for h in range(H):
            rows, cols = spot(i, h)
            arrived(q_in.at[rows, cols], dn_recv.at[i, h])

    near = jnp.where(odd == 0, 1, groups - 1)
    far = groups - near

    def ag_copy(g, k):
        there = pl.ds(own, R)
        return remote(
            lam_all.at[g, there],
            lam_all.at[g, there],
            ag_send.at[g, k - 1],
            ag_recv.at[g, k - 1],
            d,
            peer(k),
        )

    def ag_forward(g):
        there = block(near)
        return remote(
            lam_all.at[g, there],
            lam_all.at[g, there],
            ag_send.at[g, 1],
            ag_recv.at[g, 1],
            d,
            peer(near),
        )

    def ag_relay(g):
        arrived(lam_all.at[g, block(near)], ag_recv.at[g, near - 1])
        ag_forward(g).start()

    def ag_wait(g):
        arrived(lam_all.at[g, block(far)], ag_recv.at[g, far - 1])
        arrived(lam_all.at[g, block(2)], ag_recv.at[g, 1])

    def columns(k):
        return pl.ds(pl.multiple_of(peer(k) * Ks, Ks), Ks)

    def q0_copy(k, i):
        row = pl.multiple_of(i * S, S)
        return remote(
            qb.at[0, pl.ds(row, S), columns(k)],
            qs.at[0, pl.ds(pl.multiple_of(own + row, S), S)],
            q0_send.at[k - 1, i],
            q0_recv.at[k - 1, i],
            d,
            peer(k),
        )

    half = R // 2

    def part_of(k, n):
        start = lax.rem(r + groups - k, groups) * R + n * half
        return pl.ds(pl.multiple_of(start, half), half)

    def qx_copy(g, n, k):
        return remote(
            qb.at[g, pl.ds(n * half, half), columns(k)],
            qs.at[g, part_of(0, n)],
            qx_send.at[g - 1, n, k - 1],
            qx_recv.at[g - 1, n, k - 1],
            d,
            peer(k),
        )

    def qx_first(g):
        return remote(
            qb.at[g, pl.ds(0, half), columns(2)],
            relay.at[g - 1],
            qx_send.at[g - 1, 0, 1],
            rl_recv.at[g - 1],
            d,
            peer(groups - 1),
        )

    def qx_second(g):
        return remote(
            relay.at[g - 1],
            qs.at[g, part_of(groups - 1, 0)],
            rl_send.at[g - 1],
            qx_recv.at[g - 1, 0, 1],
            d,
            peer(groups - 1),
        )

    def pass_on(g):
        arrived(relay.at[g - 1], rl_recv.at[g - 1])
        qx_second(g).start()

    def qx_wait(g):
        for n in range(2):
            for k in range(1, groups):
                arrived(qs.at[g, part_of(k, n)], qx_recv.at[g - 1, n, k - 1])

    def qp_copy(j, step):
        return remote(qs.at[0], qp, qp_send.at[j], qp_recv.at[0], d + step, r)

    def tp_copy(k):
        return remote(
            q_in.at[:, columns(k)],
            qp.at[pl.ds(own, R)],
            tp_send.at[k - 1],
            tp_recv.at[k - 1],
            d,
            peer(k),
        )

    def ob_copy(k):
        return remote(observed, obs_all.at[r], ob_send.at[k - 1], ob_recv.at[k - 1], d, peer(k))

    chain = parent[2] == d * 3 + 1
    ones = jnp.ones((16, K), BF16)
    values = lax.broadcasted_iota(jnp.int32, (V, R), 0)

    def emitted(g):
        loads["e", g].wait()
        hot = jnp.where(values == observed[g : g + 1, :], 1.0, 0.0).astype(BF16)
        table = em[g]
        column = jnp.sum(table.astype(F32), axis=0, keepdims=True)
        return dot_tn(hot, table) * (1.0 / column)

    def scaled(u):
        return (u * (1.0 / jnp.mean(u, axis=1, keepdims=True))).astype(BF16)

    def lift_local(g, u):
        lam = scaled(u)
        lam_all[g, pl.ds(own, R), :] = lam
        left = jnp.concatenate([lam, ones], axis=0)
        if g > 0:
            loads["m", g].wait()
        parts = []
        for n in range(K // NB):
            cols = slice(n * NB, (n + 1) * NB)
            acc = dot_nt(left, A[g, cols, :])
            macc[g, :, cols] = acc[:R]
            parts.append(acc[:R] * (1.0 / acc[R : R + 1]))
        return parts

    parts = lift_local(2, emitted(2))
    for n, part in enumerate(parts):
        m2[:, n * NB : (n + 1) * NB] = part
    parts = lift_local(1, emitted(1) * jnp.where(chain, m2[...], 1.0))
    for n, part in enumerate(parts):
        cols = slice(n * NB, (n + 1) * NB)
        upart[:, cols] = part * jnp.where(chain, 1.0, m2[:, cols])
    upart[...] = upart[...] * emitted(0)
    loads["m", 0].wait()

    pl.semaphore_wait(barrier, lvl + (groups - 1) + jnp.where(is_root, 0, 1))

    def aux():
        for k in range(1, groups):
            ob_copy(k).start()
        for g in (2, 1):
            ag_copy(g, 1).start()
            ag_copy(g, groups - 1).start()
        for g in (2, 1):
            macc[g] = 1.0 / macc[g]

    @pl.when(lvl == 0)
    def _():
        for n, part in enumerate(lift_local(0, upart[...])):
            m_out[:, n * NB : (n + 1) * NB] = part.astype(BF16)
        for i, h in pieces:
            up_copy(i, h).start()
        ag_copy(0, 1).start()
        ag_copy(0, groups - 1).start()
        aux()
        macc[0] = 1.0 / macc[0]

    @pl.when(lvl > 0)
    def _():
        aux()
        for b in range(K // NB):
            A0T[:, b * NB : (b + 1) * NB] = A[0, b * NB : (b + 1) * NB, :].T

    def early_child(j, carry):
        for i in range(C):
            wait_up(j, i)
        upart[...] = upart[...] * msg_in[j].astype(F32)
        return carry

    lax.fori_loop(0, lvl - 1, early_child, 0)

    def up(i):
        rows = pl.ds(pl.multiple_of(i * S, S), S)

        wait_up(lvl - 1, i)
        lam = scaled(upart[rows, :] * msg_in[lvl - 1, rows, :].astype(F32))
        left = jnp.concatenate([lam, ones], axis=0)
        for h in range(H):
            cols = slice(h * W, (h + 1) * W)
            acc = dot_nn(left, A0T[:, cols])
            inverse = 1.0 / acc[S : S + 1]
            m_out[rows, cols] = (acc[:S] * inverse).astype(BF16)

            @pl.when(jnp.logical_not(is_root))
            def _():
                up_copy(i, h).start()

            inv_row[0:1, cols] = inverse
            macc[0, rows, cols] = jnp.where(is_root, acc[:S], 1.0 / acc[:S])
        lam_all[0, pl.ds(pl.multiple_of(own + i * S, S), S), :] = lam

    at_once = [(0, lvl > 1)]
    if levels > 4:
        at_once.append((3, lvl > 4))
    if levels > 5:
        at_once.append((4, lvl > 5))
    if levels > 3:
        at_once.append((2, lvl > 3))
    if levels > 2:
        at_once.append((1, lvl == 3))

    def down(i):
        row = pl.multiple_of(i * S, S)
        rows = pl.ds(row, S)

        @pl.when(is_root)
        def _():
            weight = (prior[...] / jnp.sum(prior[...], axis=1, keepdims=True)) * inv_row[0:1, :]
            joint = weight * macc[0, rows, :]
            part = 1.0 / jnp.sum(joint, axis=1, keepdims=True)
            h0[rows, :] = (weight * part).astype(BF16)
            q_in[rows, :] = (joint * part).astype(BF16)
            macc[0, rows, :] = 1.0 / macc[0, rows, :]

        @pl.when(jnp.logical_not(is_root))
        def _():
            wait_dn(i)
            h0[rows, :] = (q_in[rows, :].astype(F32) * macc[0, rows, :]).astype(BF16)

        left = h0[rows, :]
        for h in range(H):
            cols = slice(h * W, (h + 1) * W)
            lam = lam_all[0, pl.ds(pl.multiple_of(own + row, S), S), cols].astype(F32)
            q = lam * dot_nn(left, A[0, :, cols])
            qb[0, rows, cols] = q.astype(BF16)

            @pl.when(lvl > 0)
            def _():
                dn_copy(lvl - 1, low // 2, i, h).start()

            for j, test in at_once:

                @pl.when(test)
                def _(j=j):
                    dn_copy(j, 2**j, i, h).start()

            q0f[rows, cols] = q
        for k in range(1, groups):
            q0_copy(k, i).start()
        qs[0, pl.ds(pl.multiple_of(own + row, S), S), :] = qb[0, rows, pl.ds(mine, Ks)]

    def middle():
        for k in range(1, groups):
            src = lax.rem(r + groups - k, groups)
            arrived(obs_all.at[src], ob_recv.at[k - 1])
        obs_all[r] = observed[...]
        for g in range(3):
            for n in range(groups):
                oht[g, :, n * R : (n + 1) * R] = jnp.where(
                    values == obs_all[n, g : g + 1, :], 1.0, 0.0
                ).astype(BF16)
        for g in (2, 1, 0):
            ag_wait(g)
            share = A[g, pl.ds(mine, Ks), :]
            for n in range(groups):
                part = slice(n * R, (n + 1) * R)
                ginv[g, part, :] = 1.0 / dot_nt(lam_all[g, part, :], share)

    def settle_local(g, n, q_par):
        part = slice(n * half, (n + 1) * half)
        h = (q_par * macc[g, part, :]).astype(BF16)
        for b in range(K // NB):
            cols = slice(b * NB, (b + 1) * NB)
            lam = lam_all[g, part_of(0, n), cols].astype(F32)
            q = lam * dot_nn(h, A[g, :, cols])
            qb[g, part, cols] = q.astype(BF16)
            if g == 1:
                q1f[part, cols] = q
        for k in (1, groups - 1):
            qx_copy(g, n, k).start()
        if n == 0:
            qx_first(g).start()
        else:
            qx_copy(g, n, 2).start()
        qs[g, part_of(0, n), :] = qb[g, part, pl.ds(mine, Ks)]

    def settle_both(n):
        part = slice(n * half, (n + 1) * half)
        settle_local(1, n, q0f[part, :])
        settle_local(2, n, jnp.where(chain, q1f[part, :], q0f[part, :]))

    def step(s, carry):
        is_up = jnp.where(is_root, s % 2 == 0, s < C)
        i = jnp.where(is_root, s // 2, s % C)

        @pl.when(jnp.logical_and(s == C, jnp.logical_not(is_root)))
        def _():
            ag_relay(2)
            ag_relay(1)
            ag_relay(0)

            @pl.when(lvl <= 1)
            def _():
                middle()

        @pl.when(jnp.logical_and(is_up, lvl > 0))
        def _():
            up(i)

            @pl.when(i == C - 1)
            def _():
                ag_copy(0, 1).start()
                ag_copy(0, groups - 1).start()

        @pl.when(jnp.logical_not(is_up))
        def _():
            down(i)

            @pl.when(i == C // 2 - 1)
            def _():
                settle_both(0)

        return carry

    lax.fori_loop(0, 2 * C, step, 0)

    def all_sends(j, step, begin):
        for i, h in pieces:
            copy = dn_copy(j, step, i, h)
            if begin:
                copy.start()
            else:
                copy.wait_send()

    if levels > 3:

        @pl.when(lvl > 3)
        def _():
            all_sends(1, 2, True)

    @pl.when(lvl > 1)
    def _():
        for k in range(1, groups):
            tp_copy(k).start()
        qp[pl.ds(own, R), :] = q_in[:, pl.ds(mine, Ks)]

    @pl.when(is_root)
    def _():
        ag_relay(2)
        ag_relay(1)
        ag_relay(0)

    @pl.when(lvl > 1)
    def _():
        middle()

    settle_both(1)
    pass_on(1)
    pass_on(2)

    @pl.when(jnp.logical_not(is_root))
    def _():
        for i, h in pieces:
            up_copy(i, h).wait_send()

    for k in range(1, groups):
        ob_copy(k).wait_send()
    for g in range(3):
        ag_copy(g, 1).wait_send()
        ag_copy(g, groups - 1).wait_send()
        ag_forward(g).wait_send()

    @pl.when(lvl > 0)
    def _():
        all_sends(lvl - 1, low // 2, False)

    for j, test in at_once:

        @pl.when(test)
        def _(j=j):
            all_sends(j, 2**j, False)


    def finish(g, q_par):
        h = (q_par * ginv[g]).astype(BF16)
        cells = dot_tn(h, lam_all[g])
        raw = A[g, pl.ds(mine, Ks), :].astype(F32)
        pair_v[g] = (raw * cells * pair_scale).astype(BF16)

    def tally(g):
        emit_v[g] = (dot_nn(oht[g], qs[g]) * emit_scale).astype(BF16)

    for k in range(1, groups):
        for i in range(C):
            row = pl.multiple_of(lax.rem(r + groups - k, groups) * R + i * S, S)
            arrived(qs.at[0, pl.ds(row, S)], q0_recv.at[k - 1, i])
            q0_copy(k, i).wait_send()

    for j in (0, 1):

        @pl.when(lvl > j)
        def _():
            qp_copy(j, 2**j).start()

    tally(0)
    finish(1, qs[0].astype(F32))
    qx_wait(1)
    finish(2, jnp.where(chain, qs[1].astype(F32), qs[0].astype(F32)))
    tally(1)

    @pl.when(lvl > 1)
    def _():
        for k in range(1, groups):
            arrived(qp.at[block(k)], tp_recv.at[k - 1])

    @pl.when(lvl <= 1)
    def _():
        arrived(qp, qp_recv.at[0])

    finish(0, qp[...].astype(F32))
    qx_wait(2)
    tally(2)

    if levels > 3:

        @pl.when(lvl > 3)
        def _():
            all_sends(1, 2, False)

    @pl.when(lvl > 1)
    def _():
        for k in range(1, groups):
            tp_copy(k).wait_send()

    for j in (0, 1):

        @pl.when(lvl > j)
        def _():
            qp_copy(j, 2**j).wait_send()

    for g in (1, 2):
        for n in range(2):
            for k in range(1, groups):
                qx_copy(g, n, k).wait_send()
        qx_second(g).wait_send()


def store(pair_v, emit_v, pair_out, emit_out, sem):
    first = pltpu.make_async_copy(pair_v, pair_out, sem.at[0])
    second = pltpu.make_async_copy(emit_v, emit_out, sem.at[1])
    first.start()
    second.start()
    first.wait()
    second.wait()


def per_device(levels, groups, mixing, emission, prior, parent, observed):
    nodes, K, _ = mixing.shape
    V = emission.shape[1]
    R = observed.shape[1]
    Ks = K // groups
    T = groups * R
    C = CHUNKS
    H = HALVES
    dma = pltpu.SemaphoreType.DMA
    vmem = pltpu.VMEM
    in_vmem = pl.BlockSpec(memory_space=pltpu.VMEM)
    in_place = pl.BlockSpec(memory_space=pltpu.HBM)
    results = (
        jax.ShapeDtypeStruct((nodes, Ks, K), BF16),
        jax.ShapeDtypeStruct((nodes, V, Ks), BF16),
    )
    hold = functools.partial(pltpu.with_memory_space_constraint, memory_space=pltpu.HBM)
    pair_v, emit_v = pl.pallas_call(
        functools.partial(kernel, levels, groups),
        out_shape=results,
        in_specs=[
            in_place,
            in_place,
            in_vmem,
            pl.BlockSpec(memory_space=pltpu.SMEM),
            in_vmem,
        ],
        out_specs=(in_vmem, in_vmem),
        scratch_shapes=[
            vmem((nodes, K, K), BF16),
            vmem((K, K), BF16),
            vmem((nodes, V, K), BF16),
            vmem((nodes, T, K), BF16),
            vmem((R, K), F32),
            vmem((R, K), F32),
            vmem((levels, R, K), BF16),
            vmem((R, K), BF16),
            vmem((nodes, R, K), F32),
            vmem((8, K), F32),
            vmem((R, K), BF16),
            vmem((R, K), BF16),
            vmem((R, K), F32),
            vmem((R, K), F32),
            vmem((nodes, R, K), BF16),
            vmem((T, Ks), BF16),
            vmem((nodes, T, Ks), BF16),
            vmem((2, R // 2, Ks), BF16),
            vmem((nodes, T, Ks), F32),
            vmem((groups, nodes, R), jnp.int32),
            vmem((nodes, V, T), BF16),
            dma((6,)),
            dma((C, H)),
            dma((levels, C, H)),
            dma((levels, C, H)),
            dma((C, H)),
            dma((3, groups - 1)),
            dma((3, groups - 1)),
            dma((groups - 1, C)),
            dma((groups - 1, C)),
            dma((2, 2, groups - 1)),
            dma((2, 2, groups - 1)),
            dma((2,)),
            dma((2,)),
            dma((2,)),
            dma((1,)),
            dma((groups - 1,)),
            dma((groups - 1,)),
            dma((groups - 1,)),
            dma((groups - 1,)),
        ],
        compiler_params=pltpu.CompilerParams(
            collective_id=0, has_side_effects=True, vmem_limit_bytes=VMEM_BYTES
        ),
        cost_estimate=pl.CostEstimate(flops=COST_FLOPS, bytes_accessed=COST_BYTES, transcendentals=0),
        name="tree_pass",
    )(hold(mixing), hold(emission), hold(prior.reshape(1, K)), hold(parent), hold(observed))
    return pl.pallas_call(
        store,
        out_shape=results,
        in_specs=[in_vmem, in_vmem],
        out_specs=(in_place, in_place),
        scratch_shapes=[dma((2,))],
        compiler_params=pltpu.CompilerParams(vmem_limit_bytes=1024 * 1024),
        name="store_counts",
    )(pair_v, emit_v)


def solution(mesh):
    levels = mesh.shape["leaf"].bit_length() - 1
    groups = mesh.shape["rows"]
    placed = (P("leaf", None, None), P("leaf", None, None), P(), P("leaf"), P("leaf", "rows"))
    return jax.shard_map(
        functools.partial(per_device, levels, groups),
        mesh=mesh,
        in_specs=placed,
        out_specs=(P("leaf", "rows", None), P("leaf", None, "rows")),
        check_vma=False,
    )
```

```python
import functools

import jax
import jax.numpy as jnp
from jax import lax
from jax.experimental import pallas as pl
from jax.experimental.pallas import tpu as pltpu
from jax.sharding import PartitionSpec as P

F32 = jnp.float32
BF16 = jnp.bfloat16
CHUNKS = 8
COST_FLOPS = 10**9
COST_BYTES = 10**7
VMEM_BYTES = 48_000_000
NB = 256


def dot_nt(a, b):
    return lax.dot_general(a, b, (((1,), (1,)), ((), ())), preferred_element_type=F32)


def dot_nn(a, b):
    return lax.dot_general(a, b, (((1,), (0,)), ((), ())), preferred_element_type=F32)


def dot_tn(a, b):
    return lax.dot_general(a, b, (((0,), (0,)), ((), ())), preferred_element_type=F32)


def kernel(
    levels,
    groups,
    mixing,
    emission,
    prior,
    parent,
    observed,
    pair_v,
    emit_v,
    A,
    A0T,
    em,
    lam_all,
    upart,
    m2,
    msg_in,
    m_out,
    macc,
    inv_row,
    q_in,
    q0f,
    q1f,
    qb,
    qp,
    qs,
    relay,
    ginv,
    obs_all,
    oht,
    load_sem,
    up_send,
    up_recv,
    early_recv,
    dn_send,
    dn_recv,
    ag_send,
    ag_recv,
    q0_send,
    q0_recv,
    qx_send,
    qx_recv,
    rl_send,
    rl_recv,
    qp_send,
    qp_recv,
    tp_send,
    tp_recv,
    ob_send,
    ob_recv,
):
    K = A.shape[1]
    V = em.shape[1]
    R = upart.shape[0]
    Ks = K // groups
    C = CHUNKS
    S = R // C
    pair_scale = float(K * K // (R * groups))
    emit_scale = float(V * K // (R * groups))

    d = lax.axis_index("leaf")
    r = lax.axis_index("rows")
    lvl = jnp.int32(0)
    low = jnp.int32(1)
    for j in range(levels):
        zero = jnp.where(d % (2 ** (j + 1)) == 0, 1, 0)
        lvl = lvl + zero
        low = low + zero * (2**j)
    is_root = lvl == levels
    last = jnp.where(lvl == levels - 1, 1, 0)
    for j in range(levels - 1):
        last = last + jnp.where(lvl == j, (d // (2 ** (j + 1))) % 2, 0)
    odd = d % 2
    up_dev = jnp.where(is_root, d, d - low)
    slot = jnp.minimum(lvl, levels - 1)
    own = pl.multiple_of(r * R, R)
    mine = pl.multiple_of(r * Ks, Ks)

    def peer(k):
        return lax.rem(r + k, groups)

    def block(k):
        return pl.ds(pl.multiple_of(lax.rem(r + groups - k, groups) * R, R), R)

    loads = {}
    for n, g in enumerate((2, 1, 0)):
        loads["e", g] = pltpu.make_async_copy(emission.at[g], em.at[g], load_sem.at[2 * n])
        loads["m", g] = pltpu.make_async_copy(mixing.at[g], A.at[g], load_sem.at[2 * n + 1])
        loads["e", g].start()
        loads["m", g].start()

    barrier = pltpu.get_barrier_semaphore()

    def greet(leaf, rows):
        pl.semaphore_signal(
            barrier,
            inc=1,
            device_id={"leaf": leaf, "rows": rows},
            device_id_type=pl.DeviceIdType.MESH,
        )

    @pl.when(jnp.logical_not(is_root))
    def _():
        greet(up_dev, r)

    def greet_child(j, step):
        greet(d + step, r)
        return step * 2

    lax.fori_loop(0, lvl, greet_child, jnp.int32(1))
    for k in range(1, groups):
        greet(d, peer(k))

    def remote(src, dst, send_sem, recv_sem, leaf, rows):
        return pltpu.make_async_remote_copy(
            src_ref=src,
            dst_ref=dst,
            send_sem=send_sem,
            recv_sem=recv_sem,
            device_id={"leaf": leaf, "rows": rows},
            device_id_type=pl.DeviceIdType.MESH,
        )

    def arrived(ref, sem):
        remote(ref, ref, sem, sem, d, peer(1)).wait_recv()

    def sent(ref, sem):
        remote(ref, ref, sem, sem, d, peer(1)).wait_send()

    def chunk(i):
        return pl.ds(pl.multiple_of(i * S, S), S)

    def up_start(i):
        def go(recv_sem):
            remote(
                m_out.at[chunk(i)], msg_in.at[slot, chunk(i)], up_send.at[0], recv_sem, up_dev, r
            ).start()

        @pl.when(last == 1)
        def _():
            go(up_recv.at[i])

        @pl.when(last == 0)
        def _():
            go(early_recv.at[slot])

    def dn_start(j, step, i):
        remote(
            qb.at[0, chunk(i)], q_in.at[chunk(i)], dn_send.at[j], dn_recv.at[i], d + step, r
        ).start()

    near = jnp.where(odd == 0, 1, groups - 1)
    far = groups - near

    def ag_copy(g, k):
        there = pl.ds(own, R)
        return remote(
            lam_all.at[g, there],
            lam_all.at[g, there],
            ag_send.at[g],
            ag_recv.at[g, k - 1],
            d,
            peer(k),
        )

    def ag_forward(g):
        there = block(near)
        return remote(
            lam_all.at[g, there],
            lam_all.at[g, there],
            ag_send.at[g],
            ag_recv.at[g, 1],
            d,
            peer(near),
        )

    def ag_relay(g):
        arrived(lam_all.at[g, block(near)], ag_recv.at[g, near - 1])
        ag_forward(g).start()

    def ag_wait(g):
        arrived(lam_all.at[g, block(far)], ag_recv.at[g, far - 1])
        arrived(lam_all.at[g, block(2)], ag_recv.at[g, 1])

    def columns(k):
        return pl.ds(pl.multiple_of(peer(k) * Ks, Ks), Ks)

    def q0_copy(k, i, m):
        row = pl.multiple_of(i * S, S)
        return remote(
            qb.at[0, pl.ds(row, m * S), columns(k)],
            qs.at[0, pl.ds(pl.multiple_of(own + row, S), m * S)],
            q0_send.at[0],
            q0_recv.at[k - 1],
            d,
            peer(k),
        )

    half = R // 2

    def part_of(k, n):
        start = lax.rem(r + groups - k, groups) * R + n * half
        return pl.ds(pl.multiple_of(start, half), half)

    def qx_copy(g, n, k):
        return remote(
            qb.at[g, pl.ds(n * half, half), columns(k)],
            qs.at[g, part_of(0, n)],
            qx_send.at[g - 1],
            qx_recv.at[g - 1, k - 1],
            d,
            peer(k),
        )

    def qx_first(g):
        return remote(
            qb.at[g, pl.ds(0, half), columns(2)],
            relay.at[g - 1],
            qx_send.at[g - 1],
            rl_recv.at[g - 1],
            d,
            peer(groups - 1),
        )

    def qx_second(g):
        return remote(
            relay.at[g - 1],
            qs.at[g, part_of(groups - 1, 0)],
            rl_send.at[0],
            qx_recv.at[g - 1, 1],
            d,
            peer(groups - 1),
        )

    def pass_on(g):
        arrived(relay.at[g - 1], rl_recv.at[g - 1])
        qx_second(g).start()

    def qx_wait(g):
        for k in range(1, groups):
            arrived(qs.at[g, block(k)], qx_recv.at[g - 1, k - 1])

    def qp_copy(j, step):
        return remote(qs.at[0], qp, qp_send.at[0], qp_recv.at[0], d + step, r)

    def tp_copy(k):
        return remote(
            q_in.at[:, columns(k)],
            qp.at[pl.ds(own, R)],
            tp_send.at[0],
            tp_recv.at[k - 1],
            d,
            peer(k),
        )

    def ob_copy(k):
        return remote(observed, obs_all.at[r], ob_send.at[0], ob_recv.at[k - 1], d, peer(k))

    chain = parent[2] == d * 3 + 1
    ones = jnp.ones((16, K), BF16)
    values = lax.broadcasted_iota(jnp.int32, (V, R), 0)

    def emitted(g):
        loads["e", g].wait()
        hot = jnp.where(values == observed[g : g + 1, :], 1.0, 0.0).astype(BF16)
        table = em[g]
        column = jnp.sum(table.astype(F32), axis=0, keepdims=True)
        return dot_tn(hot, table) * (1.0 / column)

    def scaled(u):
        return (u * (1.0 / jnp.mean(u, axis=1, keepdims=True))).astype(BF16)

    def lift_local(g, u):
        lam = scaled(u)
        lam_all[g, pl.ds(own, R), :] = lam
        left = jnp.concatenate([lam, ones], axis=0)
        if g > 0:
            loads["m", g].wait()
        parts = []
        for n in range(K // NB):
            cols = slice(n * NB, (n + 1) * NB)
            acc = dot_nt(left, A[g, cols, :])
            macc[g, :, cols] = acc[:R]
            parts.append(acc[:R] * (1.0 / acc[R : R + 1]))
        return parts

    parts = lift_local(2, emitted(2))
    for n, part in enumerate(parts):
        m2[:, n * NB : (n + 1) * NB] = part
    parts = lift_local(1, emitted(1) * jnp.where(chain, m2[...], 1.0))
    for n, part in enumerate(parts):
        cols = slice(n * NB, (n + 1) * NB)
        upart[:, cols] = part * jnp.where(chain, 1.0, m2[:, cols])
    upart[...] = upart[...] * emitted(0)
    loads["m", 0].wait()

    pl.semaphore_wait(barrier, lvl + (groups - 1) + jnp.where(is_root, 0, 1))

    def aux():
        for k in range(1, groups):
            ob_copy(k).start()
        for g in (2, 1):
            ag_copy(g, 1).start()
            ag_copy(g, groups - 1).start()
        for g in (2, 1):
            macc[g] = 1.0 / macc[g]

    @pl.when(lvl == 0)
    def _():
        for n, part in enumerate(lift_local(0, upart[...])):
            m_out[:, n * NB : (n + 1) * NB] = part.astype(BF16)
        for i in range(C):
            up_start(i)
        ag_copy(0, 1).start()
        ag_copy(0, groups - 1).start()
        aux()
        macc[0] = 1.0 / macc[0]

    @pl.when(lvl > 0)
    def _():
        aux()
        for b in range(K // NB):
            A0T[:, b * NB : (b + 1) * NB] = A[0, b * NB : (b + 1) * NB, :].T

    def early_child(j, carry):
        arrived(msg_in.at[j], early_recv.at[j])
        upart[...] = upart[...] * msg_in[j].astype(F32)
        return carry

    lax.fori_loop(0, lvl - 1, early_child, 0)

    @pl.when(is_root)
    def _():
        ag_relay(2)
        ag_relay(1)

    def up(i, m=1):
        M = m * S
        rows = pl.ds(pl.multiple_of(i * S, S), M)
        for n in range(m):
            arrived(msg_in.at[lvl - 1, chunk(i + n)], up_recv.at[i + n])
        lam = scaled(upart[rows, :] * msg_in[lvl - 1, rows, :].astype(F32))
        acc = dot_nn(jnp.concatenate([lam, ones], axis=0), A0T[...])
        inverse = 1.0 / acc[M : M + 1]
        if m == 1:
            m_out[rows, :] = (acc[:M] * inverse).astype(BF16)
            up_start(i)
            macc[0, rows, :] = 1.0 / acc[:M]
        else:
            inv_row[0:1, :] = inverse
            macc[0, rows, :] = acc[:M]
        lam_all[0, pl.ds(pl.multiple_of(own + i * S, S), M), :] = lam

    at_once = [(0, lvl > 1)]
    if levels > 4:
        at_once.append((3, lvl > 4))

    def down(i, m=1):
        M = m * S
        row = pl.multiple_of(i * S, S)
        rows = pl.ds(row, M)
        if m == 1:
            arrived(q_in.at[rows], dn_recv.at[i])
            left = (q_in[rows, :].astype(F32) * macc[0, rows, :]).astype(BF16)
        else:
            weight = (prior[...] / jnp.sum(prior[...], axis=1, keepdims=True)) * inv_row[0:1, :]
            joint = weight * macc[0, rows, :]
            part = 1.0 / jnp.sum(joint, axis=1, keepdims=True)
            left = (weight * part).astype(BF16)
            q_in[rows, :] = (joint * part).astype(BF16)
        there = pl.ds(pl.multiple_of(own + row, S), M)
        q = lam_all[0, there, :].astype(F32) * dot_nn(left, A[0])
        qb[0, rows, :] = q.astype(BF16)
        for n in range(m):

            @pl.when(lvl > 0)
            def _():
                dn_start(lvl - 1, low // 2, i + n)

            for j, test in at_once:

                @pl.when(test)
                def _(j=j):
                    dn_start(j, 2**j, i + n)

        if m > 1 and levels > 5:
            for n in range(m):
                dn_start(4, 16, i + n)
        q0f[rows, :] = q
        for k in range(1, groups):
            q0_copy(k, i, m).start()
        qs[0, there, :] = qb[0, rows, pl.ds(mine, Ks)]

    def middle():
        for k in range(1, groups):
            src = lax.rem(r + groups - k, groups)
            arrived(obs_all.at[src], ob_recv.at[k - 1])
        obs_all[r] = observed[...]
        for g in range(3):
            for n in range(groups):
                oht[g, :, n * R : (n + 1) * R] = jnp.where(
                    values == obs_all[n, g : g + 1, :], 1.0, 0.0
                ).astype(BF16)
        for g in (2, 1, 0):
            ag_wait(g)
            share = A[g, pl.ds(mine, Ks), :]
            for n in range(groups):
                part = slice(n * R, (n + 1) * R)
                ginv[g, part, :] = 1.0 / dot_nt(lam_all[g, part, :], share)

    def settle_local(g, n, q_par):
        part = slice(n * half, (n + 1) * half)
        h = (q_par * macc[g, part, :]).astype(BF16)
        for b in range(K // NB):
            cols = slice(b * NB, (b + 1) * NB)
            lam = lam_all[g, part_of(0, n), cols].astype(F32)
            q = lam * dot_nn(h, A[g, :, cols])
            qb[g, part, cols] = q.astype(BF16)
            if g == 1:
                q1f[part, cols] = q
        for k in (1, groups - 1):
            qx_copy(g, n, k).start()
        if n == 0:
            qx_first(g).start()
        else:
            qx_copy(g, n, 2).start()
        qs[g, part_of(0, n), :] = qb[g, part, pl.ds(mine, Ks)]

    def settle_both(n):
        part = slice(n * half, (n + 1) * half)
        settle_local(1, n, q0f[part, :])
        settle_local(2, n, jnp.where(chain, q1f[part, :], q0f[part, :]))

    def gather_first():
        ag_copy(0, 1).start()
        ag_copy(0, groups - 1).start()

    @pl.when(is_root)
    def _():
        up(0, C // 2)
        down(0, C // 2)
        up(C // 2, C // 2)
        down(C // 2, C // 2)
        gather_first()

    def step(s, carry):
        @pl.when(s == C)
        def _():
            @pl.when(lvl > 0)
            def _():
                gather_first()

            ag_relay(2)
            ag_relay(1)
            ag_relay(0)

            @pl.when(lvl <= 1)
            def _():
                middle()

        @pl.when(s < C)
        def _():
            up(s)

        @pl.when(s >= C)
        def _():
            down(s - C)

            @pl.when(jnp.logical_and(s == C + C // 2 - 1, lvl <= 1))
            def _():
                settle_both(0)

        return carry

    lax.fori_loop(jnp.where(lvl == 0, C, 0), jnp.where(is_root, 0, 2 * C), step, 0)

    later = []
    if levels > 3:
        later.append((2, lvl > 3))
    if levels > 2:
        later.append((1, lvl > 2))
    for j, test in later:

        @pl.when(test)
        def _(j=j):
            for i in range(C):
                dn_start(j, 2**j, i)

    @pl.when(lvl > 1)
    def _():
        for k in range(1, groups):
            tp_copy(k).start()
        qp[pl.ds(own, R), :] = q_in[:, pl.ds(mine, Ks)]

    @pl.when(is_root)
    def _():
        ag_relay(0)

    @pl.when(lvl > 1)
    def _():
        settle_both(0)

    def share():
        for k in range(1, groups):
            arrived(qs.at[0, block(k)], q0_recv.at[k - 1])
        for j in (0, 1):

            @pl.when(lvl > j)
            def _():
                qp_copy(j, 2**j).start()

    @pl.when(lvl > 1)
    def _():
        middle()
        share()

    settle_both(1)
    pass_on(1)
    pass_on(2)

    @pl.when(jnp.logical_not(is_root))
    def _():
        sent(m_out, up_send.at[0])

    sent(obs_all.at[0 : groups - 1], ob_send.at[0])
    for g in range(3):
        sent(lam_all.at[g, 0 : 3 * R], ag_send.at[g])

    def sent_child(j, carry):
        sent(qb.at[0], dn_send.at[j])
        return carry

    lax.fori_loop(0, lvl, sent_child, 0)

    def finish(g, q_par):
        h = (q_par * ginv[g]).astype(BF16)
        cells = dot_tn(h, lam_all[g])
        raw = A[g, pl.ds(mine, Ks), :].astype(F32)
        pair_v[g] = (raw * cells * pair_scale).astype(BF16)

    def tally(g):
        emit_v[g] = (dot_nn(oht[g], qs[g]) * emit_scale).astype(BF16)

    @pl.when(lvl <= 1)
    def _():
        share()

    tally(0)
    finish(1, qs[0].astype(F32))
    @pl.when(lvl > 1)
    def _():
        for k in range(1, groups):
            arrived(qp.at[block(k)], tp_recv.at[k - 1])

    @pl.when(lvl <= 1)
    def _():
        arrived(qp, qp_recv.at[0])

    finish(0, qp[...].astype(F32))
    qx_wait(1)
    finish(2, jnp.where(chain, qs[1].astype(F32), qs[0].astype(F32)))
    tally(1)
    qx_wait(2)
    tally(2)

    three = (groups - 1) * R

    @pl.when(lvl > 1)
    def _():
        sent(qp.at[0:three], tp_send.at[0])
        sent(qs.at[0:2], qp_send.at[0])

    @pl.when(lvl == 1)
    def _():
        sent(qs.at[0], qp_send.at[0])

    sent(qs.at[0, 0:three], q0_send.at[0])
    for g in (1, 2):
        sent(qs.at[g, 0:three], qx_send.at[g - 1])
    sent(relay, rl_send.at[0])


def store(pair_v, emit_v, pair_out, emit_out, sem):
    first = pltpu.make_async_copy(pair_v, pair_out, sem.at[0])
    second = pltpu.make_async_copy(emit_v, emit_out, sem.at[1])
    first.start()
    second.start()
    first.wait()
    second.wait()


def per_device(levels, groups, mixing, emission, prior, parent, observed):
    nodes, K, _ = mixing.shape
    V = emission.shape[1]
    R = observed.shape[1]
    Ks = K // groups
    T = groups * R
    C = CHUNKS
    dma = pltpu.SemaphoreType.DMA
    vmem = pltpu.VMEM
    in_vmem = pl.BlockSpec(memory_space=pltpu.VMEM)
    in_place = pl.BlockSpec(memory_space=pltpu.HBM)
    results = (
        jax.ShapeDtypeStruct((nodes, Ks, K), BF16),
        jax.ShapeDtypeStruct((nodes, V, Ks), BF16),
    )
    hold = functools.partial(pltpu.with_memory_space_constraint, memory_space=pltpu.HBM)
    pair_v, emit_v = pl.pallas_call(
        functools.partial(kernel, levels, groups),
        out_shape=results,
        in_specs=[
            in_place,
            in_place,
            in_vmem,
            pl.BlockSpec(memory_space=pltpu.SMEM),
            in_vmem,
        ],
        out_specs=(in_vmem, in_vmem),
        scratch_shapes=[
            vmem((nodes, K, K), BF16),
            vmem((K, K), BF16),
            vmem((nodes, V, K), BF16),
            vmem((nodes, T, K), BF16),
            vmem((R, K), F32),
            vmem((R, K), F32),
            vmem((levels, R, K), BF16),
            vmem((R, K), BF16),
            vmem((nodes, R, K), F32),
            vmem((8, K), F32),
            vmem((R, K), BF16),
            vmem((R, K), F32),
            vmem((R, K), F32),
            vmem((nodes, R, K), BF16),
            vmem((T, Ks), BF16),
            vmem((nodes, T, Ks), BF16),
            vmem((2, R // 2, Ks), BF16),
            vmem((nodes, T, Ks), F32),
            vmem((groups, nodes, R), jnp.int32),
            vmem((nodes, V, T), BF16),
            dma((6,)),
            dma((1,)),
            dma((C,)),
            dma((levels,)),
            dma((levels,)),
            dma((C,)),
            dma((nodes,)),
            dma((nodes, groups - 1)),
            dma((1,)),
            dma((groups - 1,)),
            dma((2,)),
            dma((2, groups - 1)),
            dma((1,)),
            dma((2,)),
            dma((1,)),
            dma((1,)),
            dma((1,)),
            dma((groups - 1,)),
            dma((1,)),
            dma((groups - 1,)),
        ],
        compiler_params=pltpu.CompilerParams(
            collective_id=0, has_side_effects=True, vmem_limit_bytes=VMEM_BYTES
        ),
        cost_estimate=pl.CostEstimate(flops=COST_FLOPS, bytes_accessed=COST_BYTES, transcendentals=0),
        name="tree_pass",
    )(hold(mixing), hold(emission), hold(prior.reshape(1, K)), hold(parent), hold(observed))
    return pl.pallas_call(
        store,
        out_shape=results,
        in_specs=[in_vmem, in_vmem],
        out_specs=(in_place, in_place),
        scratch_shapes=[dma((2,))],
        compiler_params=pltpu.CompilerParams(vmem_limit_bytes=1024 * 1024),
        name="store_counts",
    )(pair_v, emit_v)


def solution(mesh):
    levels = mesh.shape["leaf"].bit_length() - 1
    groups = mesh.shape["rows"]
    placed = (P("leaf", None, None), P("leaf", None, None), P(), P("leaf"), P("leaf", "rows"))
    return jax.shard_map(
        functools.partial(per_device, levels, groups),
        mesh=mesh,
        in_specs=placed,
        out_specs=(P("leaf", "rows", None), P("leaf", None, "rows")),
        check_vma=False,
    )
```

```python
import functools

import jax
import jax.numpy as jnp
from jax import lax
from jax.experimental import pallas as pl
from jax.experimental.pallas import tpu as pltpu
from jax.sharding import PartitionSpec as P

F32 = jnp.float32
BF16 = jnp.bfloat16
CHUNKS = 8
COST_FLOPS = 10**9
COST_BYTES = 10**7
VMEM_BYTES = 48_000_000
NB = 256


def dot_nt(a, b):
    return lax.dot_general(a, b, (((1,), (1,)), ((), ())), preferred_element_type=F32)


def dot_nn(a, b):
    return lax.dot_general(a, b, (((1,), (0,)), ((), ())), preferred_element_type=F32)


def dot_tn(a, b):
    return lax.dot_general(a, b, (((0,), (0,)), ((), ())), preferred_element_type=F32)


def kernel(
    levels,
    groups,
    mixing,
    emission,
    prior,
    parent,
    observed,
    pair_v,
    emit_v,
    A,
    A0T,
    em,
    lam_all,
    upart,
    m2,
    msg_in,
    m_out,
    macc,
    inv_row,
    q_in,
    q0f,
    q1f,
    qb,
    qp,
    qs,
    relay,
    ginv,
    obs_all,
    oht,
    load_sem,
    up_send,
    up_recv,
    early_recv,
    dn_send,
    dn_recv,
    ag_send,
    ag_recv,
    q0_send,
    q0_recv,
    qx_send,
    qx_recv,
    rl_send,
    rl_recv,
    qp_send,
    qp_recv,
    tp_send,
    tp_recv,
    ob_send,
    ob_recv,
):
    K = A.shape[1]
    V = em.shape[1]
    R = upart.shape[0]
    Ks = K // groups
    C = CHUNKS
    S = R // C
    pair_scale = float(K * K // (R * groups))
    emit_scale = float(V * K // (R * groups))

    d = lax.axis_index("leaf")
    r = lax.axis_index("rows")
    lvl = jnp.int32(0)
    low = jnp.int32(1)
    for j in range(levels):
        zero = jnp.where(d % (2 ** (j + 1)) == 0, 1, 0)
        lvl = lvl + zero
        low = low + zero * (2**j)
    is_root = lvl == levels
    last = jnp.where(lvl == levels - 1, 1, 0)
    for j in range(levels - 1):
        last = last + jnp.where(lvl == j, (d // (2 ** (j + 1))) % 2, 0)
    odd = d % 2
    up_dev = jnp.where(is_root, d, d - low)
    slot = jnp.minimum(lvl, levels - 1)
    own = pl.multiple_of(r * R, R)
    mine = pl.multiple_of(r * Ks, Ks)

    def peer(k):
        return lax.rem(r + k, groups)

    def block(k):
        return pl.ds(pl.multiple_of(lax.rem(r + groups - k, groups) * R, R), R)

    loads = {}
    for n, g in enumerate((2, 1, 0)):
        loads["e", g] = pltpu.make_async_copy(emission.at[g], em.at[g], load_sem.at[2 * n])
        loads["m", g] = pltpu.make_async_copy(mixing.at[g], A.at[g], load_sem.at[2 * n + 1])
    for kind in ("e", "m"):
        for g in (2, 1, 0):
            loads[kind, g].start()

    barrier = pltpu.get_barrier_semaphore()

    def greet(leaf, rows):
        pl.semaphore_signal(
            barrier,
            inc=1,
            device_id={"leaf": leaf, "rows": rows},
            device_id_type=pl.DeviceIdType.MESH,
        )

    @pl.when(jnp.logical_not(is_root))
    def _():
        greet(up_dev, r)

    def greet_child(j, step):
        greet(d + step, r)
        return step * 2

    lax.fori_loop(0, lvl, greet_child, jnp.int32(1))
    for k in range(1, groups):
        greet(d, peer(k))

    def remote(src, dst, send_sem, recv_sem, leaf, rows):
        return pltpu.make_async_remote_copy(
            src_ref=src,
            dst_ref=dst,
            send_sem=send_sem,
            recv_sem=recv_sem,
            device_id={"leaf": leaf, "rows": rows},
            device_id_type=pl.DeviceIdType.MESH,
        )

    def arrived(ref, sem):
        remote(ref, ref, sem, sem, d, peer(1)).wait_recv()

    def sent(ref, sem):
        remote(ref, ref, sem, sem, d, peer(1)).wait_send()

    def chunk(i):
        return pl.ds(pl.multiple_of(i * S, S), S)

    def up_start(i):
        def go(recv_sem):
            remote(
                m_out.at[chunk(i)], msg_in.at[slot, chunk(i)], up_send.at[0], recv_sem, up_dev, r
            ).start()

        @pl.when(last == 1)
        def _():
            go(up_recv.at[i])

        @pl.when(last == 0)
        def _():
            go(early_recv.at[slot])

    def dn_start(j, step, i):
        remote(
            qb.at[0, chunk(i)], q_in.at[chunk(i)], dn_send.at[j], dn_recv.at[i], d + step, r
        ).start()

    near = jnp.where(odd == 0, 1, groups - 1)
    far = groups - near

    def ag_copy(g, k):
        there = pl.ds(own, R)
        return remote(
            lam_all.at[g, there],
            lam_all.at[g, there],
            ag_send.at[g],
            ag_recv.at[g, k - 1],
            d,
            peer(k),
        )

    def ag_forward(g):
        there = block(near)
        return remote(
            lam_all.at[g, there],
            lam_all.at[g, there],
            ag_send.at[g],
            ag_recv.at[g, 1],
            d,
            peer(near),
        )

    def ag_relay(g):
        arrived(lam_all.at[g, block(near)], ag_recv.at[g, near - 1])
        ag_forward(g).start()

    def ag_wait(g):
        arrived(lam_all.at[g, block(far)], ag_recv.at[g, far - 1])
        arrived(lam_all.at[g, block(2)], ag_recv.at[g, 1])

    def columns(k):
        return pl.ds(pl.multiple_of(peer(k) * Ks, Ks), Ks)

    def q0_copy(k, i, m):
        row = pl.multiple_of(i * S, S)
        return remote(
            qb.at[0, pl.ds(row, m * S), columns(k)],
            qs.at[0, pl.ds(pl.multiple_of(own + row, S), m * S)],
            q0_send.at[0],
            q0_recv.at[k - 1],
            d,
            peer(k),
        )

    half = R // 2

    def part_of(k, n):
        start = lax.rem(r + groups - k, groups) * R + n * half
        return pl.ds(pl.multiple_of(start, half), half)

    def qx_copy(g, n, k):
        return remote(
            qb.at[g, pl.ds(n * half, half), columns(k)],
            qs.at[g, part_of(0, n)],
            qx_send.at[g - 1],
            qx_recv.at[g - 1, k - 1],
            d,
            peer(k),
        )

    def qx_first(g):
        return remote(
            qb.at[g, pl.ds(0, half), columns(2)],
            relay.at[g - 1],
            qx_send.at[g - 1],
            rl_recv.at[g - 1],
            d,
            peer(groups - 1),
        )

    def qx_second(g):
        return remote(
            relay.at[g - 1],
            qs.at[g, part_of(groups - 1, 0)],
            rl_send.at[0],
            qx_recv.at[g - 1, 1],
            d,
            peer(groups - 1),
        )

    def pass_on(g):
        arrived(relay.at[g - 1], rl_recv.at[g - 1])
        qx_second(g).start()

    def qx_wait(g):
        for k in range(1, groups):
            arrived(qs.at[g, block(k)], qx_recv.at[g - 1, k - 1])

    def qp_copy(j, step):
        return remote(qs.at[0], qp, qp_send.at[0], qp_recv.at[0], d + step, r)

    def tp_copy(k):
        return remote(
            q_in.at[:, columns(k)],
            qp.at[pl.ds(own, R)],
            tp_send.at[0],
            tp_recv.at[k - 1],
            d,
            peer(k),
        )

    def ob_copy(k):
        return remote(observed, obs_all.at[r], ob_send.at[0], ob_recv.at[k - 1], d, peer(k))

    chain = parent[2] == d * 3 + 1
    ones = jnp.ones((16, K), BF16)
    values = lax.broadcasted_iota(jnp.int32, (V, R), 0)

    def emitted(g):
        loads["e", g].wait()
        hot = jnp.where(values == observed[g : g + 1, :], 1.0, 0.0).astype(BF16)
        table = em[g]
        column = jnp.sum(table.astype(F32), axis=0, keepdims=True)
        return dot_tn(hot, table) * (1.0 / column)

    def scaled(u):
        return (u * (1.0 / jnp.mean(u, axis=1, keepdims=True))).astype(BF16)

    def lift_local(g, u):
        lam = scaled(u)
        lam_all[g, pl.ds(own, R), :] = lam
        left = jnp.concatenate([lam, ones], axis=0)
        loads["m", g].wait()
        parts = []
        for n in range(K // NB):
            cols = slice(n * NB, (n + 1) * NB)
            acc = dot_nt(left, A[g, cols, :])
            macc[g, :, cols] = acc[:R]
            parts.append(acc[:R] * (1.0 / acc[R : R + 1]))
        return parts

    first = emitted(2)
    q1f[...] = emitted(1)
    upart[...] = emitted(0)
    parts = lift_local(2, first)
    for n, part in enumerate(parts):
        m2[:, n * NB : (n + 1) * NB] = part
    parts = lift_local(1, q1f[...] * jnp.where(chain, m2[...], 1.0))
    for n, part in enumerate(parts):
        cols = slice(n * NB, (n + 1) * NB)
        upart[:, cols] = upart[:, cols] * part * jnp.where(chain, 1.0, m2[:, cols])
    loads["m", 0].wait()

    pl.semaphore_wait(barrier, lvl + (groups - 1) + jnp.where(is_root, 0, 1))

    def aux():
        for k in range(1, groups):
            ob_copy(k).start()
        for g in (2, 1):
            ag_copy(g, 1).start()
            ag_copy(g, groups - 1).start()
        for g in (2, 1):
            macc[g] = 1.0 / macc[g]

    @pl.when(lvl == 0)
    def _():
        for n in range(2):
            part = slice(n * half, (n + 1) * half)
            lam = scaled(upart[part, :])
            lam_all[0, part_of(0, n), :] = lam
            left = jnp.concatenate([lam, ones], axis=0)
            for b in range(K // NB):
                cols = slice(b * NB, (b + 1) * NB)
                acc = dot_nt(left, A[0, cols, :])
                macc[0, part, cols] = acc[:half]
                m_out[part, cols] = (acc[:half] * (1.0 / acc[half : half + 1])).astype(BF16)
            for i in range(n * C // 2, (n + 1) * C // 2):
                up_start(i)
        ag_copy(0, 1).start()
        ag_copy(0, groups - 1).start()
        aux()
        macc[0] = 1.0 / macc[0]

    @pl.when(lvl > 0)
    def _():
        aux()
        for b in range(K // NB):
            A0T[:, b * NB : (b + 1) * NB] = A[0, b * NB : (b + 1) * NB, :].T
        inv_row[...] = 1.0 / dot_nn(ones, A0T[...])[:8]

    def early_child(j, carry):
        arrived(msg_in.at[j], early_recv.at[j])
        upart[...] = upart[...] * msg_in[j].astype(F32)
        return carry

    lax.fori_loop(0, lvl - 1, early_child, 0)

    @pl.when(is_root)
    def _():
        ag_relay(2)
        ag_relay(1)

    def up(i, m=1):
        M = m * S
        rows = pl.ds(pl.multiple_of(i * S, S), M)
        for n in range(m):
            arrived(msg_in.at[lvl - 1, chunk(i + n)], up_recv.at[i + n])
        lam = scaled(upart[rows, :] * msg_in[lvl - 1, rows, :].astype(F32))
        acc = dot_nn(lam, A0T[...])
        if m == 1:
            m_out[rows, :] = (acc * inv_row[0:1, :]).astype(BF16)
            up_start(i)
            macc[0, rows, :] = 1.0 / acc
        else:
            macc[0, rows, :] = acc
        lam_all[0, pl.ds(pl.multiple_of(own + i * S, S), M), :] = lam

    at_once = [(0, lvl > 1)]
    if levels > 4:
        at_once.append((3, lvl > 4))

    def down(i, m=1, root=False):
        M = m * S
        row = pl.multiple_of(i * S, S)
        rows = pl.ds(row, M)
        if not root:
            for n in range(m):
                arrived(q_in.at[chunk(i + n)], dn_recv.at[i + n])
            left = (q_in[rows, :].astype(F32) * macc[0, rows, :]).astype(BF16)
        else:
            weight = (prior[...] / jnp.sum(prior[...], axis=1, keepdims=True)) * inv_row[0:1, :]
            joint = weight * macc[0, rows, :]
            part = 1.0 / jnp.sum(joint, axis=1, keepdims=True)
            left = (weight * part).astype(BF16)
            q_in[rows, :] = (joint * part).astype(BF16)
        there = pl.ds(pl.multiple_of(own + row, S), M)
        q = lam_all[0, there, :].astype(F32) * dot_nn(left, A[0])
        qb[0, rows, :] = q.astype(BF16)
        for n in range(m if m == 1 or root else 0):

            @pl.when(lvl > 0)
            def _():
                dn_start(lvl - 1, low // 2, i + n)

            for j, test in at_once:

                @pl.when(test)
                def _(j=j):
                    dn_start(j, 2**j, i + n)

        if root and levels > 5:
            for n in range(m):
                dn_start(4, 16, i + n)
        q0f[rows, :] = q
        for k in range(1, groups):
            q0_copy(k, i, m).start()
        qs[0, there, :] = qb[0, rows, pl.ds(mine, Ks)]

    def middle():
        for k in range(1, groups):
            src = lax.rem(r + groups - k, groups)
            arrived(obs_all.at[src], ob_recv.at[k - 1])
        obs_all[r] = observed[...]
        for g in range(3):
            for n in range(groups):
                oht[g, :, n * R : (n + 1) * R] = jnp.where(
                    values == obs_all[n, g : g + 1, :], 1.0, 0.0
                ).astype(BF16)
        for g in (2, 1, 0):
            ag_wait(g)
            share = A[g, pl.ds(mine, Ks), :]
            for n in range(groups):
                part = slice(n * R, (n + 1) * R)
                ginv[g, part, :] = 1.0 / dot_nt(lam_all[g, part, :], share)

    def settle_local(g, n, q_par):
        part = slice(n * half, (n + 1) * half)
        h = (q_par * macc[g, part, :]).astype(BF16)
        for b in range(K // NB):
            cols = slice(b * NB, (b + 1) * NB)
            lam = lam_all[g, part_of(0, n), cols].astype(F32)
            q = lam * dot_nn(h, A[g, :, cols])
            qb[g, part, cols] = q.astype(BF16)
            if g == 1:
                q1f[part, cols] = q
        for k in (1, groups - 1):
            qx_copy(g, n, k).start()
        if n == 0:
            qx_first(g).start()
        else:
            qx_copy(g, n, 2).start()
        qs[g, part_of(0, n), :] = qb[g, part, pl.ds(mine, Ks)]

    def settle_both(n):
        part = slice(n * half, (n + 1) * half)
        settle_local(1, n, q0f[part, :])
        settle_local(2, n, jnp.where(chain, q1f[part, :], q0f[part, :]))

    def gather_first():
        ag_copy(0, 1).start()
        ag_copy(0, groups - 1).start()

    @pl.when(is_root)
    def _():
        up(0, C // 2)
        down(0, C // 2, True)
        up(C // 2, C // 2)
        down(C // 2, C // 2, True)
        gather_first()

    def step(s, carry):
        @pl.when(s == C)
        def _():
            @pl.when(lvl > 0)
            def _():
                gather_first()

            ag_relay(2)
            ag_relay(1)
            ag_relay(0)

            @pl.when(lvl <= 1)
            def _():
                middle()

        @pl.when(s < C)
        def _():
            up(s)

        @pl.when(jnp.logical_and(s >= C, lvl > 0))
        def _():
            down(s - C)

            @pl.when(jnp.logical_and(s == C + C // 2 - 1, lvl == 1))
            def _():
                settle_both(0)

        @pl.when(jnp.logical_and(s == C, lvl == 0))
        def _():
            down(0, C // 2)
            settle_both(0)
            down(C // 2, C // 2)

        return carry

    lax.fori_loop(jnp.where(lvl == 0, C, 0), jnp.where(is_root, 0, 2 * C), step, 0)

    later = []
    if levels > 3:
        later.append((2, lvl > 3))
    if levels > 2:
        later.append((1, lvl > 2))
    for j, test in later:

        @pl.when(test)
        def _(j=j):
            for i in range(C):
                dn_start(j, 2**j, i)

    @pl.when(lvl > 1)
    def _():
        for k in range(1, groups):
            tp_copy(k).start()
        qp[pl.ds(own, R), :] = q_in[:, pl.ds(mine, Ks)]

    @pl.when(is_root)
    def _():
        ag_relay(0)

    @pl.when(lvl > 1)
    def _():
        settle_both(0)

    def share():
        for k in range(1, groups):
            arrived(qs.at[0, block(k)], q0_recv.at[k - 1])
        for j in (0, 1):

            @pl.when(lvl > j)
            def _():
                qp_copy(j, 2**j).start()

    @pl.when(lvl > 1)
    def _():
        middle()
        share()

    settle_both(1)
    pass_on(1)
    pass_on(2)

    @pl.when(jnp.logical_not(is_root))
    def _():
        sent(m_out, up_send.at[0])

    sent(obs_all.at[0 : groups - 1], ob_send.at[0])
    for g in range(3):
        sent(lam_all.at[g, 0 : 3 * R], ag_send.at[g])

    def sent_child(j, carry):
        sent(qb.at[0], dn_send.at[j])
        return carry

    lax.fori_loop(0, lvl, sent_child, 0)

    def finish(g, q_par):
        h = (q_par * ginv[g]).astype(BF16)
        cells = dot_tn(h, lam_all[g])
        raw = A[g, pl.ds(mine, Ks), :].astype(F32)
        pair_v[g] = (raw * cells * pair_scale).astype(BF16)

    def tally(g):
        emit_v[g] = (dot_nn(oht[g], qs[g]) * emit_scale).astype(BF16)

    @pl.when(lvl <= 1)
    def _():
        share()

    tally(0)
    finish(1, qs[0].astype(F32))
    @pl.when(lvl > 1)
    def _():
        for k in range(1, groups):
            arrived(qp.at[block(k)], tp_recv.at[k - 1])

    @pl.when(lvl <= 1)
    def _():
        arrived(qp, qp_recv.at[0])

    finish(0, qp[...].astype(F32))
    qx_wait(1)
    finish(2, jnp.where(chain, qs[1].astype(F32), qs[0].astype(F32)))
    tally(1)
    qx_wait(2)
    tally(2)

    three = (groups - 1) * R

    @pl.when(lvl > 1)
    def _():
        sent(qp.at[0:three], tp_send.at[0])
        sent(qs.at[0:2], qp_send.at[0])

    @pl.when(lvl == 1)
    def _():
        sent(qs.at[0], qp_send.at[0])

    sent(qs.at[0, 0:three], q0_send.at[0])
    for g in (1, 2):
        sent(qs.at[g, 0:three], qx_send.at[g - 1])
    sent(relay, rl_send.at[0])


def store(pair_v, emit_v, pair_out, emit_out, sem):
    first = pltpu.make_async_copy(pair_v, pair_out, sem.at[0])
    second = pltpu.make_async_copy(emit_v, emit_out, sem.at[1])
    first.start()
    second.start()
    first.wait()
    second.wait()


def per_device(levels, groups, mixing, emission, prior, parent, observed):
    nodes, K, _ = mixing.shape
    V = emission.shape[1]
    R = observed.shape[1]
    Ks = K // groups
    T = groups * R
    C = CHUNKS
    dma = pltpu.SemaphoreType.DMA
    vmem = pltpu.VMEM
    in_vmem = pl.BlockSpec(memory_space=pltpu.VMEM)
    in_place = pl.BlockSpec(memory_space=pltpu.HBM)
    results = (
        jax.ShapeDtypeStruct((nodes, Ks, K), BF16),
        jax.ShapeDtypeStruct((nodes, V, Ks), BF16),
    )
    hold = functools.partial(pltpu.with_memory_space_constraint, memory_space=pltpu.HBM)
    pair_v, emit_v = pl.pallas_call(
        functools.partial(kernel, levels, groups),
        out_shape=results,
        in_specs=[
            in_place,
            in_place,
            in_vmem,
            pl.BlockSpec(memory_space=pltpu.SMEM),
            in_vmem,
        ],
        out_specs=(in_vmem, in_vmem),
        scratch_shapes=[
            vmem((nodes, K, K), BF16),
            vmem((K, K), BF16),
            vmem((nodes, V, K), BF16),
            vmem((nodes, T, K), BF16),
            vmem((R, K), F32),
            vmem((R, K), F32),
            vmem((levels, R, K), BF16),
            vmem((R, K), BF16),
            vmem((nodes, R, K), F32),
            vmem((8, K), F32),
            vmem((R, K), BF16),
            vmem((R, K), F32),
            vmem((R, K), F32),
            vmem((nodes, R, K), BF16),
            vmem((T, Ks), BF16),
            vmem((nodes, T, Ks), BF16),
            vmem((2, R // 2, Ks), BF16),
            vmem((nodes, T, Ks), F32),
            vmem((groups, nodes, R), jnp.int32),
            vmem((nodes, V, T), BF16),
            dma((6,)),
            dma((1,)),
            dma((C,)),
            dma((levels,)),
            dma((levels,)),
            dma((C,)),
            dma((nodes,)),
            dma((nodes, groups - 1)),
            dma((1,)),
            dma((groups - 1,)),
            dma((2,)),
            dma((2, groups - 1)),
            dma((1,)),
            dma((2,)),
            dma((1,)),
            dma((1,)),
            dma((1,)),
            dma((groups - 1,)),
            dma((1,)),
            dma((groups - 1,)),
        ],
        compiler_params=pltpu.CompilerParams(
            collective_id=0, has_side_effects=True, vmem_limit_bytes=VMEM_BYTES
        ),
        cost_estimate=pl.CostEstimate(flops=COST_FLOPS, bytes_accessed=COST_BYTES, transcendentals=0),
        name="tree_pass",
    )(hold(mixing), hold(emission), hold(prior.reshape(1, K)), hold(parent), hold(observed))
    return pl.pallas_call(
        store,
        out_shape=results,
        in_specs=[in_vmem, in_vmem],
        out_specs=(in_place, in_place),
        scratch_shapes=[dma((2,))],
        compiler_params=pltpu.CompilerParams(vmem_limit_bytes=1024 * 1024),
        name="store_counts",
    )(pair_v, emit_v)


def solution(mesh):
    levels = mesh.shape["leaf"].bit_length() - 1
    groups = mesh.shape["rows"]
    placed = (P("leaf", None, None), P("leaf", None, None), P(), P("leaf"), P("leaf", "rows"))
    return jax.shard_map(
        functools.partial(per_device, levels, groups),
        mesh=mesh,
        in_specs=placed,
        out_specs=(P("leaf", "rows", None), P("leaf", None, "rows")),
        check_vma=False,
    )
```

```python
import functools

import jax
import jax.numpy as jnp
from jax import lax
from jax.experimental import pallas as pl
from jax.experimental.pallas import tpu as pltpu
from jax.sharding import PartitionSpec as P

F32 = jnp.float32
BF16 = jnp.bfloat16
CHUNKS = 8
COST_FLOPS = 10**9
COST_BYTES = 10**7
VMEM_BYTES = 48_000_000
NB = 256


def dot_nt(a, b):
    return lax.dot_general(a, b, (((1,), (1,)), ((), ())), preferred_element_type=F32)


def dot_nn(a, b):
    return lax.dot_general(a, b, (((1,), (0,)), ((), ())), preferred_element_type=F32)


def dot_tn(a, b):
    return lax.dot_general(a, b, (((0,), (0,)), ((), ())), preferred_element_type=F32)


def kernel(
    levels,
    groups,
    mixing,
    emission,
    prior,
    parent,
    observed,
    pair_v,
    emit_v,
    A,
    A0T,
    em,
    lam_all,
    upart,
    m2,
    msg_in,
    m_out,
    macc,
    inv_row,
    q_in,
    q0f,
    q1f,
    qb,
    qp,
    qs,
    relay,
    ginv,
    obs_all,
    oht,
    load_sem,
    up_send,
    up_recv,
    early_recv,
    dn_send,
    dn_recv,
    ag_send,
    ag_recv,
    q0_send,
    q0_recv,
    qx_send,
    qx_recv,
    rl_send,
    rl_recv,
    qp_send,
    qp_recv,
    tp_send,
    tp_recv,
    ob_send,
    ob_recv,
):
    K = A.shape[1]
    V = em.shape[1]
    R = upart.shape[0]
    Ks = K // groups
    C = CHUNKS
    S = R // C
    pair_scale = float(K * K // (R * groups))
    emit_scale = float(V * K // (R * groups))

    d = lax.axis_index("leaf")
    r = lax.axis_index("rows")
    lvl = jnp.int32(0)
    low = jnp.int32(1)
    for j in range(levels):
        zero = jnp.where(d % (2 ** (j + 1)) == 0, 1, 0)
        lvl = lvl + zero
        low = low + zero * (2**j)
    is_root = lvl == levels
    last = jnp.where(lvl == levels - 1, 1, 0)
    for j in range(levels - 1):
        last = last + jnp.where(lvl == j, (d // (2 ** (j + 1))) % 2, 0)
    odd = d % 2
    up_dev = jnp.where(is_root, d, d - low)
    slot = jnp.minimum(lvl, levels - 1)
    own = pl.multiple_of(r * R, R)
    mine = pl.multiple_of(r * Ks, Ks)

    def peer(k):
        return lax.rem(r + k, groups)

    def block(k):
        return pl.ds(pl.multiple_of(lax.rem(r + groups - k, groups) * R, R), R)

    loads = {}
    for n, g in enumerate((2, 1, 0)):
        loads["e", g] = pltpu.make_async_copy(emission.at[g], em.at[g], load_sem.at[2 * n])
        loads["m", g] = pltpu.make_async_copy(mixing.at[g], A.at[g], load_sem.at[2 * n + 1])
    for kind in ("e", "m"):
        for g in (2, 1, 0):
            loads[kind, g].start()

    barrier = pltpu.get_barrier_semaphore()

    def greet(leaf, rows):
        pl.semaphore_signal(
            barrier,
            inc=1,
            device_id={"leaf": leaf, "rows": rows},
            device_id_type=pl.DeviceIdType.MESH,
        )

    @pl.when(jnp.logical_not(is_root))
    def _():
        greet(up_dev, r)

    def greet_child(j, step):
        greet(d + step, r)
        return step * 2

    lax.fori_loop(0, lvl, greet_child, jnp.int32(1))
    for k in range(1, groups):
        greet(d, peer(k))

    def remote(src, dst, send_sem, recv_sem, leaf, rows):
        return pltpu.make_async_remote_copy(
            src_ref=src,
            dst_ref=dst,
            send_sem=send_sem,
            recv_sem=recv_sem,
            device_id={"leaf": leaf, "rows": rows},
            device_id_type=pl.DeviceIdType.MESH,
        )

    def arrived(ref, sem):
        remote(ref, ref, sem, sem, d, peer(1)).wait_recv()

    def sent(ref, sem):
        remote(ref, ref, sem, sem, d, peer(1)).wait_send()

    def chunk(i):
        return pl.ds(pl.multiple_of(i * S, S), S)

    def up_start(i):
        def go(recv_sem):
            remote(
                m_out.at[chunk(i)], msg_in.at[slot, chunk(i)], up_send.at[0], recv_sem, up_dev, r
            ).start()

        @pl.when(last == 1)
        def _():
            go(up_recv.at[i])

        @pl.when(last == 0)
        def _():
            go(early_recv.at[slot])

    def dn_start(j, step, i):
        remote(
            qb.at[0, chunk(i)], q_in.at[chunk(i)], dn_send.at[j], dn_recv.at[i], d + step, r
        ).start()

    near = jnp.where(odd == 0, 1, groups - 1)
    far = groups - near

    def ag_copy(g, k):
        there = pl.ds(own, R)
        return remote(
            lam_all.at[g, there],
            lam_all.at[g, there],
            ag_send.at[g],
            ag_recv.at[g, k - 1],
            d,
            peer(k),
        )

    def ag_forward(g):
        there = block(near)
        return remote(
            lam_all.at[g, there],
            lam_all.at[g, there],
            ag_send.at[g],
            ag_recv.at[g, 1],
            d,
            peer(near),
        )

    def ag_relay(g):
        arrived(lam_all.at[g, block(near)], ag_recv.at[g, near - 1])
        ag_forward(g).start()

    def ag_wait(g):
        arrived(lam_all.at[g, block(far)], ag_recv.at[g, far - 1])
        arrived(lam_all.at[g, block(2)], ag_recv.at[g, 1])

    def columns(k):
        return pl.ds(pl.multiple_of(peer(k) * Ks, Ks), Ks)

    def q0_copy(k, i, m):
        row = pl.multiple_of(i * S, S)
        return remote(
            qb.at[0, pl.ds(row, m * S), columns(k)],
            qs.at[0, pl.ds(pl.multiple_of(own + row, S), m * S)],
            q0_send.at[0],
            q0_recv.at[k - 1],
            d,
            peer(k),
        )

    half = R // 2

    def part_of(k, n):
        start = lax.rem(r + groups - k, groups) * R + n * half
        return pl.ds(pl.multiple_of(start, half), half)

    def qx_copy(g, n, k):
        return remote(
            qb.at[g, pl.ds(n * half, half), columns(k)],
            qs.at[g, part_of(0, n)],
            qx_send.at[g - 1],
            qx_recv.at[g - 1, k - 1],
            d,
            peer(k),
        )

    def qx_first(g):
        return remote(
            qb.at[g, pl.ds(0, half), columns(2)],
            relay.at[g - 1],
            qx_send.at[g - 1],
            rl_recv.at[g - 1],
            d,
            peer(groups - 1),
        )

    def qx_second(g):
        return remote(
            relay.at[g - 1],
            qs.at[g, part_of(groups - 1, 0)],
            rl_send.at[0],
            qx_recv.at[g - 1, 1],
            d,
            peer(groups - 1),
        )

    def pass_on(g):
        arrived(relay.at[g - 1], rl_recv.at[g - 1])
        qx_second(g).start()

    def qx_wait(g):
        for k in range(1, groups):
            arrived(qs.at[g, block(k)], qx_recv.at[g - 1, k - 1])

    def qp_copy(j, step):
        return remote(qs.at[0], qp, qp_send.at[0], qp_recv.at[0], d + step, r)

    def tp_copy(k):
        return remote(
            q_in.at[:, columns(k)],
            qp.at[pl.ds(own, R)],
            tp_send.at[0],
            tp_recv.at[k - 1],
            d,
            peer(k),
        )

    def ob_copy(k):
        return remote(observed, obs_all.at[r], ob_send.at[0], ob_recv.at[k - 1], d, peer(k))

    chain = parent[2] == d * 3 + 1
    ones = jnp.ones((16, K), BF16)
    values = lax.broadcasted_iota(jnp.int32, (V, R), 0)

    def emitted(g):
        loads["e", g].wait()
        hot = jnp.where(values == observed[g : g + 1, :], 1.0, 0.0).astype(BF16)
        table = em[g]
        column = jnp.sum(table.astype(F32), axis=0, keepdims=True)
        return dot_tn(hot, table) * (1.0 / column)

    def scaled(u):
        return (u * (1.0 / jnp.mean(u, axis=1, keepdims=True))).astype(BF16)

    def lift_local(g, u):
        lam = scaled(u)
        lam_all[g, pl.ds(own, R), :] = lam
        left = jnp.concatenate([lam, ones], axis=0)
        loads["m", g].wait()
        parts = []
        for n in range(K // NB):
            cols = slice(n * NB, (n + 1) * NB)
            acc = dot_nt(left, A[g, cols, :])
            macc[g, :, cols] = acc[:R]
            parts.append(acc[:R] * (1.0 / acc[R : R + 1]))
        return parts

    first = emitted(2)
    q1f[...] = emitted(1)
    upart[...] = emitted(0)
    parts = lift_local(2, first)
    for n, part in enumerate(parts):
        m2[:, n * NB : (n + 1) * NB] = part
    parts = lift_local(1, q1f[...] * jnp.where(chain, m2[...], 1.0))
    for n, part in enumerate(parts):
        cols = slice(n * NB, (n + 1) * NB)
        upart[:, cols] = upart[:, cols] * part * jnp.where(chain, 1.0, m2[:, cols])
    loads["m", 0].wait()

    pl.semaphore_wait(barrier, lvl + (groups - 1) + jnp.where(is_root, 0, 1))

    def aux():
        for k in range(1, groups):
            ob_copy(k).start()
        for g in (2, 1):
            ag_copy(g, 1).start()
            ag_copy(g, groups - 1).start()
        for g in (2, 1):
            macc[g] = 1.0 / macc[g]

    @pl.when(lvl == 0)
    def _():
        for n in range(2):
            part = slice(n * half, (n + 1) * half)
            lam = scaled(upart[part, :])
            lam_all[0, part_of(0, n), :] = lam
            left = jnp.concatenate([lam, ones], axis=0)
            for b in range(K // NB):
                cols = slice(b * NB, (b + 1) * NB)
                acc = dot_nt(left, A[0, cols, :])
                macc[0, part, cols] = acc[:half]
                m_out[part, cols] = (acc[:half] * (1.0 / acc[half : half + 1])).astype(BF16)
            for i in range(n * C // 2, (n + 1) * C // 2):
                up_start(i)
        ag_copy(0, 1).start()
        ag_copy(0, groups - 1).start()
        aux()
        macc[0] = 1.0 / macc[0]

    @pl.when(lvl > 0)
    def _():
        aux()
        for b in range(K // NB):
            A0T[:, b * NB : (b + 1) * NB] = A[0, b * NB : (b + 1) * NB, :].T
        inv_row[...] = 1.0 / dot_nn(ones, A0T[...])[:8]

    def early_child(j, carry):
        arrived(msg_in.at[j], early_recv.at[j])
        upart[...] = upart[...] * msg_in[j].astype(F32)
        return carry

    lax.fori_loop(0, lvl - 1, early_child, 0)

    @pl.when(is_root)
    def _():
        ag_relay(2)
        ag_relay(1)

    def up(i, m=1):
        M = m * S
        rows = pl.ds(pl.multiple_of(i * S, S), M)
        for n in range(m):
            arrived(msg_in.at[lvl - 1, chunk(i + n)], up_recv.at[i + n])
        lam = scaled(upart[rows, :] * msg_in[lvl - 1, rows, :].astype(F32))
        acc = dot_nn(lam, A0T[...])
        if m == 1:
            m_out[rows, :] = (acc * inv_row[0:1, :]).astype(BF16)
            up_start(i)
            macc[0, rows, :] = 1.0 / acc
        else:
            macc[0, rows, :] = acc
        lam_all[0, pl.ds(pl.multiple_of(own + i * S, S), M), :] = lam

    at_once = [(0, lvl > 1)]
    if levels > 4:
        at_once.append((3, lvl > 4))
    if levels > 3:
        at_once.append((2, lvl > 3))
    if levels > 2:
        at_once.append((1, lvl == 3))

    def down(i, m=1, root=False):
        M = m * S
        row = pl.multiple_of(i * S, S)
        rows = pl.ds(row, M)
        if not root:
            for n in range(m):
                arrived(q_in.at[chunk(i + n)], dn_recv.at[i + n])
            left = (q_in[rows, :].astype(F32) * macc[0, rows, :]).astype(BF16)
        else:
            weight = (prior[...] / jnp.sum(prior[...], axis=1, keepdims=True)) * inv_row[0:1, :]
            joint = weight * macc[0, rows, :]
            part = 1.0 / jnp.sum(joint, axis=1, keepdims=True)
            left = (weight * part).astype(BF16)
            q_in[rows, :] = (joint * part).astype(BF16)
        there = pl.ds(pl.multiple_of(own + row, S), M)
        q = lam_all[0, there, :].astype(F32) * dot_nn(left, A[0])
        qb[0, rows, :] = q.astype(BF16)
        for n in range(m if m == 1 or root else 0):

            @pl.when(lvl > 0)
            def _():
                dn_start(lvl - 1, low // 2, i + n)

            for j, test in at_once:

                @pl.when(test)
                def _(j=j):
                    dn_start(j, 2**j, i + n)

        if root and levels > 5:
            for n in range(m):
                dn_start(4, 16, i + n)
        q0f[rows, :] = q
        for k in range(1, groups):
            q0_copy(k, i, m).start()
        qs[0, there, :] = qb[0, rows, pl.ds(mine, Ks)]

    def middle():
        for k in range(1, groups):
            src = lax.rem(r + groups - k, groups)
            arrived(obs_all.at[src], ob_recv.at[k - 1])
        obs_all[r] = observed[...]
        for g in range(3):
            for n in range(groups):
                oht[g, :, n * R : (n + 1) * R] = jnp.where(
                    values == obs_all[n, g : g + 1, :], 1.0, 0.0
                ).astype(BF16)
        for g in (2, 1, 0):
            ag_wait(g)
            share = A[g, pl.ds(mine, Ks), :]
            for n in range(groups):
                part = slice(n * R, (n + 1) * R)
                ginv[g, part, :] = 1.0 / dot_nt(lam_all[g, part, :], share)

    def settle_local(g, n, q_par):
        part = slice(n * half, (n + 1) * half)
        h = (q_par * macc[g, part, :]).astype(BF16)
        for b in range(K // NB):
            cols = slice(b * NB, (b + 1) * NB)
            lam = lam_all[g, part_of(0, n), cols].astype(F32)
            q = lam * dot_nn(h, A[g, :, cols])
            qb[g, part, cols] = q.astype(BF16)
            if g == 1:
                q1f[part, cols] = q
        for k in (1, groups - 1):
            qx_copy(g, n, k).start()
        if n == 0:
            qx_first(g).start()
        else:
            qx_copy(g, n, 2).start()
        qs[g, part_of(0, n), :] = qb[g, part, pl.ds(mine, Ks)]

    def settle_both(n):
        part = slice(n * half, (n + 1) * half)
        settle_local(1, n, q0f[part, :])
        settle_local(2, n, jnp.where(chain, q1f[part, :], q0f[part, :]))

    def gather_first():
        ag_copy(0, 1).start()
        ag_copy(0, groups - 1).start()

    @pl.when(is_root)
    def _():
        for b in range(4):
            up(b * C // 4, C // 4)
            down(b * C // 4, C // 4, True)
        gather_first()

    def step(s, carry):
        @pl.when(s == C)
        def _():
            @pl.when(lvl > 0)
            def _():
                gather_first()

            ag_relay(2)
            ag_relay(1)
            ag_relay(0)

            @pl.when(lvl <= 1)
            def _():
                middle()

        @pl.when(s < C)
        def _():
            up(s)

        @pl.when(jnp.logical_and(s >= C, lvl > 0))
        def _():
            down(s - C)

            @pl.when(jnp.logical_and(s == C + C // 2 - 1, lvl == 1))
            def _():
                settle_both(0)

        @pl.when(jnp.logical_and(s == C, lvl == 0))
        def _():
            down(0, C // 2)
            settle_both(0)
            down(C // 2, C // 2)

        return carry

    lax.fori_loop(jnp.where(lvl == 0, C, 0), jnp.where(is_root, 0, 2 * C), step, 0)

    later = []
    if levels > 2:
        later.append((1, lvl > 3))
    for j, test in later:

        @pl.when(test)
        def _(j=j):
            for i in range(C):
                dn_start(j, 2**j, i)

    @pl.when(lvl > 1)
    def _():
        for k in range(1, groups):
            tp_copy(k).start()
        qp[pl.ds(own, R), :] = q_in[:, pl.ds(mine, Ks)]

    @pl.when(is_root)
    def _():
        ag_relay(0)

    @pl.when(lvl > 1)
    def _():
        settle_both(0)

    def share():
        for k in range(1, groups):
            arrived(qs.at[0, block(k)], q0_recv.at[k - 1])
        for j in (0, 1):

            @pl.when(lvl > j)
            def _():
                qp_copy(j, 2**j).start()

    @pl.when(lvl > 1)
    def _():
        middle()
        share()

    settle_both(1)
    pass_on(1)
    pass_on(2)

    @pl.when(jnp.logical_not(is_root))
    def _():
        sent(m_out, up_send.at[0])

    sent(obs_all.at[0 : groups - 1], ob_send.at[0])
    for g in range(3):
        sent(lam_all.at[g, 0 : 3 * R], ag_send.at[g])

    def sent_child(j, carry):
        sent(qb.at[0], dn_send.at[j])
        return carry

    lax.fori_loop(0, lvl, sent_child, 0)

    def finish(g, q_par):
        h = (q_par * ginv[g]).astype(BF16)
        cells = dot_tn(h, lam_all[g])
        raw = A[g, pl.ds(mine, Ks), :].astype(F32)
        pair_v[g] = (raw * cells * pair_scale).astype(BF16)

    def tally(g):
        emit_v[g] = (dot_nn(oht[g], qs[g]) * emit_scale).astype(BF16)

    @pl.when(lvl <= 1)
    def _():
        share()

    tally(0)
    finish(1, qs[0].astype(F32))
    @pl.when(lvl > 1)
    def _():
        for k in range(1, groups):
            arrived(qp.at[block(k)], tp_recv.at[k - 1])

    @pl.when(lvl <= 1)
    def _():
        arrived(qp, qp_recv.at[0])

    finish(0, qp[...].astype(F32))
    qx_wait(1)
    finish(2, jnp.where(chain, qs[1].astype(F32), qs[0].astype(F32)))
    tally(1)
    qx_wait(2)
    tally(2)

    three = (groups - 1) * R

    @pl.when(lvl > 1)
    def _():
        sent(qp.at[0:three], tp_send.at[0])
        sent(qs.at[0:2], qp_send.at[0])

    @pl.when(lvl == 1)
    def _():
        sent(qs.at[0], qp_send.at[0])

    sent(qs.at[0, 0:three], q0_send.at[0])
    for g in (1, 2):
        sent(qs.at[g, 0:three], qx_send.at[g - 1])
    sent(relay, rl_send.at[0])


def store(pair_v, emit_v, pair_out, emit_out, sem):
    first = pltpu.make_async_copy(pair_v, pair_out, sem.at[0])
    second = pltpu.make_async_copy(emit_v, emit_out, sem.at[1])
    first.start()
    second.start()
    first.wait()
    second.wait()


def per_device(levels, groups, mixing, emission, prior, parent, observed):
    nodes, K, _ = mixing.shape
    V = emission.shape[1]
    R = observed.shape[1]
    Ks = K // groups
    T = groups * R
    C = CHUNKS
    dma = pltpu.SemaphoreType.DMA
    vmem = pltpu.VMEM
    in_vmem = pl.BlockSpec(memory_space=pltpu.VMEM)
    in_place = pl.BlockSpec(memory_space=pltpu.HBM)
    results = (
        jax.ShapeDtypeStruct((nodes, Ks, K), BF16),
        jax.ShapeDtypeStruct((nodes, V, Ks), BF16),
    )
    hold = functools.partial(pltpu.with_memory_space_constraint, memory_space=pltpu.HBM)
    pair_v, emit_v = pl.pallas_call(
        functools.partial(kernel, levels, groups),
        out_shape=results,
        in_specs=[
            in_place,
            in_place,
            in_vmem,
            pl.BlockSpec(memory_space=pltpu.SMEM),
            in_vmem,
        ],
        out_specs=(in_vmem, in_vmem),
        scratch_shapes=[
            vmem((nodes, K, K), BF16),
            vmem((K, K), BF16),
            vmem((nodes, V, K), BF16),
            vmem((nodes, T, K), BF16),
            vmem((R, K), F32),
            vmem((R, K), F32),
            vmem((levels, R, K), BF16),
            vmem((R, K), BF16),
            vmem((nodes, R, K), F32),
            vmem((8, K), F32),
            vmem((R, K), BF16),
            vmem((R, K), F32),
            vmem((R, K), F32),
            vmem((nodes, R, K), BF16),
            vmem((T, Ks), BF16),
            vmem((nodes, T, Ks), BF16),
            vmem((2, R // 2, Ks), BF16),
            vmem((nodes, T, Ks), F32),
            vmem((groups, nodes, R), jnp.int32),
            vmem((nodes, V, T), BF16),
            dma((6,)),
            dma((1,)),
            dma((C,)),
            dma((levels,)),
            dma((levels,)),
            dma((C,)),
            dma((nodes,)),
            dma((nodes, groups - 1)),
            dma((1,)),
            dma((groups - 1,)),
            dma((2,)),
            dma((2, groups - 1)),
            dma((1,)),
            dma((2,)),
            dma((1,)),
            dma((1,)),
            dma((1,)),
            dma((groups - 1,)),
            dma((1,)),
            dma((groups - 1,)),
        ],
        compiler_params=pltpu.CompilerParams(
            collective_id=0, has_side_effects=True, vmem_limit_bytes=VMEM_BYTES
        ),
        cost_estimate=pl.CostEstimate(flops=COST_FLOPS, bytes_accessed=COST_BYTES, transcendentals=0),
        name="tree_pass",
    )(hold(mixing), hold(emission), hold(prior.reshape(1, K)), hold(parent), hold(observed))
    return pl.pallas_call(
        store,
        out_shape=results,
        in_specs=[in_vmem, in_vmem],
        out_specs=(in_place, in_place),
        scratch_shapes=[dma((2,))],
        compiler_params=pltpu.CompilerParams(vmem_limit_bytes=1024 * 1024),
        name="store_counts",
    )(pair_v, emit_v)


def solution(mesh):
    levels = mesh.shape["leaf"].bit_length() - 1
    groups = mesh.shape["rows"]
    placed = (P("leaf", None, None), P("leaf", None, None), P(), P("leaf"), P("leaf", "rows"))
    return jax.shard_map(
        functools.partial(per_device, levels, groups),
        mesh=mesh,
        in_specs=placed,
        out_specs=(P("leaf", "rows", None), P("leaf", None, "rows")),
        check_vma=False,
    )
```
